256 devices in a mesh: dp: 32 (over z, x_hi, core), slab: 8 (over y, x_lo).
Axes of the slice: x: 4 (x_hi: 2, x_lo: 2; x = x_hi * 2 + x_lo), y: 4, z: 8, core: 2. Of those that a mesh axis runs over, the one named last changes fastest.
Arguments:
- point_feats: bfloat16 [32, 128, 64, 128], P('dp', 'slab'), may hold values from -6 to 6
- point_coords: bfloat16 [32, 128, 3, 128], P('dp', 'slab'), may hold values from 0 to 1
- slot_block: int32 [32, 8, 8, 4], P('dp', 'slab'), may hold values from 0 to 15
- slot_cell: int32 [32, 8, 8, 4], P('dp', 'slab'), may hold values from 0 to 2047, as said below
- slot_count: int32 [32, 8, 8], P('dp', 'slab'), may hold values from 1 to 4, as said below
- cotangent: float32 [32, 16, 16, 16, 128], P('dp', 'slab'), may hold values from -6 to 6
- offset_map: float32 [64, 3], replicated, may hold values from -12 to 12
- offset_bias: float32 [64], replicated, may hold values from -4 to 4
- kernel_mix: bfloat16 [64, 64, 64], replicated, may hold values from -0.75 to 0.75
- lift_weight: bfloat16 [64, 64], replicated, may hold values from -0.75 to 0.75
Outputs:
- spectral_grad: float32 [64, 16, 16, 16, 128], P('dp', 'slab')
The draws below stay inside these ranges and needn't reach their ends.
Inputs may be any that keep to these rules, and one draw needn't show every extreme that they name: `slot_cell`: cell row of a slot on its receiving slab index. `slot_count`: in every sample one receiving slab index, drawn from the seed, gets 4 live slots from every sending slab index.
All inputs are finite; a program needn't handle non-finite values.
Results may differ from the reference program's by a relative error of at most 0.0031.
Values may be sent and summed in bfloat16 or wider, within the bound.
A program may use at most 64 MiB of HBM per device.

```python
import math
import jax
import jax.numpy as jnp
from jax import lax

C = 64
GX = 128
GY = 128
GZ = 128
KM = 16
BP = 128
KH = 64
CAP = 4
XL = 16
PB_DEV = 16
PBLOCKS = 128
SAMPLES = 32
N_SLAB = 8


def draw_slot_cell(key, part):
    pool_size = max(2, N_SLAB * CAP // 2)
    pool = jax.random.randint(jax.random.fold_in(key, 11), (SAMPLES, 1, N_SLAB, pool_size), 0, XL * GY)
    pool = pool.at[:, :, :, 0].set(XL * GY - 1)
    pool = pool.at[:, :, :, 1].set(0)
    picks = jax.random.randint(jax.random.fold_in(key, 12), (SAMPLES, N_SLAB, N_SLAB, CAP), 0, pool_size)
    picks = picks.at[:, 0, :, 0].set(0)
    picks = picks.at[:, 1, :, 0].set(1)
    pool_all = jnp.broadcast_to(pool, (SAMPLES, N_SLAB, N_SLAB, pool_size))
    return jnp.take_along_axis(pool_all, picks, axis=3).astype(jnp.int32)


def draw_slot_count(key, part):
    upper = max(2, CAP * 2 // 3 + 1)
    base_count = jax.random.randint(jax.random.fold_in(key, 21), (SAMPLES, N_SLAB, N_SLAB), 1, upper)
    hottest = jax.random.randint(jax.random.fold_in(key, 22), (SAMPLES, 1, 1), 0, N_SLAB)
    receivers = jnp.arange(N_SLAB)[None, None, :]
    return jnp.where(receivers == hottest, CAP, base_count).astype(jnp.int32)


def with_ends(result, key, least, top_value):
    longest = result.shape.index(max(result.shape))
    spots = []
    for shift in (0, 1):
        where = [jax.random.randint(jax.random.fold_in(key, axis), (), 0, length) for axis, length in enumerate(result.shape)]
        where[longest] = (where[longest] + shift) % result.shape[longest]
        spots.append(tuple(where))
    return result.at[spots[0]].set(least).at[spots[1]].set(top_value)


def level_of(rng, dims, pieces, least, largest):
    def one(position, shards_of):
        draws = jax.random.uniform(jax.random.fold_in(jax.random.fold_in(rng, 6), position), (shards_of,), jnp.float32, least / len(pieces), largest / len(pieces))
        return jnp.repeat(jnp.exp(draws), dims[position] // shards_of).reshape((-1,) + (1,) * (len(dims) - position - 1))

    gain = one(*pieces[0])
    for cut in pieces[1:]:
        gain = gain * one(*cut)
    return gain


def normal_values(stream_key, dims, width, most, shards=(), kind=jnp.bfloat16):
    entries = width * jax.random.normal(stream_key, dims, jnp.float32)
    if shards:
        entries = entries * level_of(stream_key, dims, shards, -0.22, 0.18)
    return jnp.clip(entries, -most, most).astype(kind)


def setup_inputs(seed: int = 0) -> dict:
    splits = jax.random.split(jax.random.key(seed), 11)
    return {
        "point_feats": normal_values(splits[0], (SAMPLES, PBLOCKS, C, BP), 1.0, 6.0, ((0, 32), (1, 8))),
        "point_coords": jnp.clip(1.0 * jax.random.uniform(splits[1], (SAMPLES, PBLOCKS, 3, BP), jnp.float32) ** level_of(splits[1], (SAMPLES, PBLOCKS, 3, BP), ((0, 32), (1, 8)), -0.2, 0.2), 0.0, 1.0).astype(jnp.bfloat16),
        "slot_block": with_ends(jax.random.randint(splits[2], (SAMPLES, N_SLAB, N_SLAB, CAP), 0, PB_DEV), jax.random.fold_in(splits[2], 1), 0, PB_DEV - 1).astype(jnp.int32),
        "slot_cell": draw_slot_cell(jax.random.fold_in(splits[10], 71), 0),
        "slot_count": draw_slot_count(jax.random.fold_in(splits[10], 71), 0),
        "cotangent": normal_values(splits[5], (SAMPLES, KM, KM, KM, 2 * C), 1.0, 6.0, ((0, 32), (1, 8)), jnp.float32),
        "offset_map": normal_values(splits[6], (KH, 3), 3.0, 12.0, (), jnp.float32),
        "offset_bias": normal_values(splits[7], (KH,), 1.0, 4.0, (), jnp.float32),
        "kernel_mix": normal_values(splits[8], (KH, C, C), C ** -0.5, 0.75),
        "lift_weight": normal_values(splits[9], (C, C), C ** -0.5, 0.75),
    }


def slot_kernel(mixed_feats, coords, cell_x, cell_y, offset_map, offset_bias):
    pos_z = (jnp.arange(GZ).astype(jnp.float32) + 0.5) / GZ
    pos_x = (cell_x.astype(jnp.float32) + 0.5) / GX
    pos_y = (cell_y.astype(jnp.float32) + 0.5) / GY
    coef_x = offset_map[:, 0][:, None]
    coef_y = offset_map[:, 1][:, None]
    coef_z = offset_map[:, 2][:, None]
    cell_part = coef_x * pos_x + coef_y * pos_y + coef_z * pos_z[None, :]
    points_f = coords.astype(jnp.float32)
    point_part = coef_x * points_f[0][None, :] + coef_y * points_f[1][None, :] + coef_z * points_f[2][None, :]
    weights = jax.nn.relu(cell_part[:, :, None] - point_part[:, None, :] + offset_bias[:, None, None]).astype(jnp.bfloat16)
    flat_weights = jnp.transpose(weights, (1, 0, 2)).reshape(GZ, KH * BP)
    slot_sum = jnp.dot(flat_weights, mixed_feats.reshape(KH * BP, C), preferred_element_type=jnp.float32) * (1.0 / BP)
    return slot_sum.reshape(GZ * C)

def spectral_modes(slot_terms, cell_ids, cell_x, cell_y, lift_weight, spec_scale):
    slot_total = cell_ids.shape[0]
    is_live = cell_ids >= 0
    same_cell = (cell_ids[:, None] == cell_ids[None, :]) & is_live[None, :]
    slot_index = jnp.arange(slot_total, dtype=jnp.int32)
    before = same_cell & (slot_index[None, :] < slot_index[:, None])
    leader = (is_live & jnp.logical_not(jnp.any(before, axis=1))).astype(jnp.float32)
    summed = jnp.dot(same_cell.astype(jnp.float32), slot_terms, precision=lax.Precision.HIGHEST, preferred_element_type=jnp.float32)
    latent = summed.astype(jnp.bfloat16).reshape(slot_total * GZ, C)
    lifted = jax.nn.gelu(jnp.dot(latent, lift_weight, preferred_element_type=jnp.float32)).reshape(slot_total, GZ, C)
    lifted = lifted * leader[:, None, None]
    cells_z = jnp.arange(GZ, dtype=jnp.int32)
    mode_freq = jnp.arange(KM, dtype=jnp.int32)
    z_turn = jnp.mod(cells_z[:, None] * mode_freq[None, :], GZ).astype(jnp.float32) * (2.0 * math.pi / GZ)
    z_table = jnp.concatenate([jnp.cos(z_turn), -jnp.sin(z_turn)], axis=1)
    z_modes = jnp.einsum('nzc,zk->nkc', lifted, z_table, precision=lax.Precision.HIGHEST, preferred_element_type=jnp.float32)
    real_z = z_modes[:, :KM].reshape(slot_total, KM * C)
    imag_z = z_modes[:, KM:].reshape(slot_total, KM * C)
    signed = jnp.where(mode_freq < KM // 2, mode_freq, mode_freq - KM)
    step_x = jnp.mod(cell_x[:, None].astype(jnp.int32) * signed[None, :], GX).astype(jnp.float32)
    step_y = jnp.mod(cell_y[:, None].astype(jnp.int32) * signed[None, :], GY).astype(jnp.float32)
    phase_angle = (step_x[:, :, None] / GX + step_y[:, None, :] / GY) * (2.0 * math.pi)
    phase_angle = phase_angle.reshape(slot_total, KM * KM)
    cos_part = jnp.cos(phase_angle)
    sin_part = -jnp.sin(phase_angle)
    contract = (((0,), (0,)), ((), ()))
    high = lax.Precision.HIGHEST
    real_x = lax.dot_general(cos_part, real_z, contract, precision=high, preferred_element_type=jnp.float32) - lax.dot_general(sin_part, imag_z, contract, precision=high, preferred_element_type=jnp.float32)
    imag_x = lax.dot_general(cos_part, imag_z, contract, precision=high, preferred_element_type=jnp.float32) + lax.dot_general(sin_part, real_z, contract, precision=high, preferred_element_type=jnp.float32)
    out_shape = (KM, KM, KM, C)
    return jnp.concatenate([real_x.reshape(out_shape), imag_x.reshape(out_shape)], axis=3) * spec_scale

def sample_modes(feats, coords, blocks, cells, counts, offset_map, offset_bias, kernel_mix, lift_weight):
    planes = GX // N_SLAB
    mixed_all = jnp.einsum('ncp,hcd->nhpd', feats.astype(jnp.float32), kernel_mix.astype(jnp.float32), precision=lax.Precision.HIGHEST).astype(jnp.bfloat16)
    src_index = jnp.arange(N_SLAB, dtype=jnp.int32)[:, None, None]
    dst_index = jnp.arange(N_SLAB, dtype=jnp.int32)[None, :, None]
    slot_order = jnp.arange(CAP, dtype=jnp.int32)[None, None, :]
    is_live = slot_order < counts[:, :, None]
    block_ids = (src_index * PB_DEV + blocks).reshape(-1).astype(jnp.int32)
    cell_x = (dst_index * planes + cells // GY).reshape(-1).astype(jnp.int32)
    cell_y = (cells % GY).reshape(-1).astype(jnp.int32)
    cell_ids = jnp.where(is_live, dst_index * (planes * GY) + cells, -1).reshape(-1).astype(jnp.int32)

    def one_slot(slot_args):
        block_id, row_x, row_y = slot_args
        return slot_kernel(mixed_all[block_id], coords[block_id], row_x, row_y, offset_map, offset_bias)
    slot_terms = lax.map(one_slot, (block_ids, cell_x, cell_y))
    spec_scale = 1.0 / math.sqrt(GZ * N_SLAB * N_SLAB * CAP)
    return spectral_modes(slot_terms, cell_ids, cell_x, cell_y, lift_weight, spec_scale)

def reference(point_feats, point_coords, slot_block, slot_cell, slot_count, cotangent, offset_map, offset_bias, kernel_mix, lift_weight):

    def per_sample(sample_args):
        feats, coords, blocks, cells, counts = sample_args
        return sample_modes(feats, coords, blocks, cells, counts, offset_map, offset_bias, kernel_mix, lift_weight)
    all_modes = lax.map(per_sample, (point_feats, point_coords, slot_block, slot_cell, slot_count))
    real_modes = all_modes[..., :C]
    imag_modes = all_modes[..., C:]
    grad_real = cotangent[..., :C]
    grad_imag = cotangent[..., C:]
    left_side = jnp.concatenate([grad_real, grad_imag], axis=4)
    right_side = jnp.concatenate([grad_imag, -grad_real], axis=4)
    high = lax.Precision.HIGHEST
    first_sum = jnp.einsum('bxyzi,bxyzo->ixyzo', real_modes, left_side, precision=high)
    second_sum = jnp.einsum('bxyzi,bxyzo->ixyzo', imag_modes, right_side, precision=high)
    return first_sum + second_sum
```

```python
import math

import jax
import jax.numpy as jnp
import numpy as np
from jax import lax
from jax.experimental import pallas as pl
from jax.experimental.pallas import tpu as pltpu
from jax.sharding import PartitionSpec as P

F32 = jnp.float32
BF16 = jnp.bfloat16
NT = (((1,), (1,)), ((), ()))
VMEM_BYTES = 60 * 2**20


def split(x):
    hi = x.astype(BF16)
    return hi, (x - hi.astype(F32)).astype(BF16)


def dot3(a, b):
    ah, al = a
    bh, bl = b
    out = jnp.dot(ah, bh, preferred_element_type=F32)
    out = out + jnp.dot(al, bh, preferred_element_type=F32)
    return out + jnp.dot(ah, bl, preferred_element_type=F32)


def np_split(x):
    hi = np.asarray(x, np.float32).astype(BF16)
    lo = (np.asarray(x, np.float64) - hi.astype(np.float64)).astype(BF16)
    return hi, lo


def tables():
    z = np.arange(128)
    k = np.arange(16)
    turn = np.mod(z[:, None] * k[None, :], 128) * (2.0 * np.pi / 128)
    z_table = np.tile(np.concatenate([np.cos(turn), -np.sin(turn)], axis=1), (1, 8))
    z_hi, z_lo = np_split(z_table)
    signed = np.where(k < 8, k, k - 16)
    angle = np.mod(signed[:, None] * z[None, :], 128) * (2.0 * np.pi / 128)
    by_x = np.repeat(angle, 16, axis=0)
    by_y = np.tile(angle, (16, 1))
    xy = []
    for part in (np.cos(by_x), np.sin(by_x), np.cos(by_y), np.sin(by_y)):
        xy.append(np.concatenate(np_split(part), axis=1))
    return z_hi, z_lo, np.concatenate(xy, axis=0)


def terms_kernel(blk, cel, cnt, om, feats, coords, mix, coef, lift, out, mixed, tab, base, lifted, live, todo, seen):
    for b in range(16):
        seen[b] = 0

    def scan(n, carry):
        n_live, n_todo = carry
        slab = n // 4
        is_live = (n - slab * 4) < cnt[slab]
        b = blk[n]
        fresh = jnp.logical_and(is_live, seen[b] == 0)
        live[n_live] = n
        todo[n_todo] = b
        seen[b] = jnp.where(is_live, 1, seen[b])
        return n_live + is_live.astype(jnp.int32), n_todo + fresh.astype(jnp.int32)

    n_live, n_todo = lax.fori_loop(0, 32, scan, (jnp.int32(0), jnp.int32(0)))
    lifted[...] = jnp.zeros_like(lifted)
    pos_z = (lax.broadcasted_iota(jnp.int32, (128, 128), 0).astype(F32) + 0.5) * (1.0 / 128)

    def fill(h, carry):
        tab[h] = pos_z * om[h * 3 + 2]
        return carry

    lax.fori_loop(0, 64, fill, 0)

    def mix_pair(i, carry):
        b0 = todo[2 * i]
        b1 = todo[jnp.minimum(2 * i + 1, n_todo - 1)]
        pair = jnp.concatenate([feats[b0], feats[b1]], axis=1)

        def rows(r, carry):
            start = pl.multiple_of(r * 512, 512)
            m = jnp.dot(mix[pl.ds(start, 512), :], pair, preferred_element_type=F32).astype(BF16)
            mixed[b0, pl.ds(start, 512), :] = m[:, :128]
            mixed[b1, pl.ds(start, 512), :] = m[:, 128:]
            return carry

        return lax.fori_loop(0, 8, rows, carry)

    lax.fori_loop(0, (n_todo + 1) // 2, mix_pair, 0)
    coef_x, coef_y, coef_z, bias = (coef[:, c : c + 1] for c in range(4))
    lift_v = lift[...]

    def slot(i, carry):
        n = live[i]
        b = blk[n]
        cell = cel[n]
        x = (n // 4) * 16 + cell // 128
        y = lax.rem(cell, 128)
        pos_x = (x.astype(F32) + 0.5) * (1.0 / 128)
        pos_y = (y.astype(F32) + 0.5) * (1.0 / 128)
        q = coords[b].astype(F32)
        point = coef_x * q[0:1] + coef_y * q[1:2] + coef_z * q[2:3]
        base[...] = (coef_x * pos_x + coef_y * pos_y) + bias - point
        ws, ms = [], []
        for h in range(64):
            w = (tab[h] + base[pl.ds(h, 1), :]).astype(BF16)
            ws.append(jnp.maximum(w, jnp.zeros_like(w)))
            ms.append(mixed[b, h * 64 : (h + 1) * 64, :])
        total = lax.dot_general(
            jnp.concatenate(ws, axis=1), jnp.concatenate(ms, axis=1), NT, preferred_element_type=F32
        )
        hi, lo = split(total.T * (1.0 / 128))
        pre = jnp.dot(lift_v, hi, preferred_element_type=F32) + jnp.dot(lift_v, lo, preferred_element_type=F32)
        lifted[pl.ds(pl.multiple_of(n * 64, 64), 64), :] = pre
        return carry

    lax.fori_loop(0, n_live, slot, 0)
    for e in range(64):
        out[e // 8, e % 8] = lifted[pl.ds(e, 32, stride=64), :].astype(BF16)


def lifted_terms(blk, cel, cnt, om, feats, coords, mix, coef, lift):
    sm = pl.BlockSpec(memory_space=pltpu.SMEM)
    vm = pl.BlockSpec(memory_space=pltpu.VMEM)
    return pl.pallas_call(
        terms_kernel,
        out_shape=jax.ShapeDtypeStruct((8, 8, 32, 128), BF16),
        in_specs=[sm] * 4 + [vm] * 5,
        out_specs=vm,
        scratch_shapes=[
            pltpu.VMEM((16, 4096, 128), BF16),
            pltpu.VMEM((64, 128, 128), F32),
            pltpu.VMEM((64, 128), F32),
            pltpu.VMEM((32 * 64, 128), F32),
            pltpu.SMEM((33,), jnp.int32),
            pltpu.SMEM((33,), jnp.int32),
            pltpu.SMEM((16,), jnp.int32),
        ],
        compiler_params=pltpu.CompilerParams(vmem_limit_bytes=VMEM_BYTES),
        cost_estimate=pl.CostEstimate(flops=4 * 10**9, bytes_accessed=2 * 2**20, transcendentals=0),
        name="slot_terms",
    )(blk, cel, cnt, om, feats, coords, mix, coef, lift)


def modes_value(tag_col, tag_row, terms, z_hi, z_lo, xy):
    lane = lax.broadcasted_iota(jnp.int32, (256, 256), 1)
    row = lax.broadcasted_iota(jnp.int32, (256, 256), 0)
    same = jnp.logical_and(tag_col == tag_row, tag_row >= 0)
    before = jnp.logical_and(same, lane < row)
    early = jnp.max(jnp.where(before, 1.0, 0.0), axis=1, keepdims=True)
    leader = jnp.where(tag_col[:, :1] >= 0, 1.0 - early, 0.0)
    sums = jnp.dot(jnp.where(same, 1.0, 0.0).astype(BF16), terms, preferred_element_type=F32)
    inner = math.sqrt(2.0 / math.pi) * (sums + 0.044715 * (sums * sums * sums))
    acts = (0.5 * leader) * (sums * (1.0 + jnp.tanh(inner)))
    z_lane = lax.broadcasted_iota(jnp.int32, (128, 256), 1) // 32
    zero = jnp.zeros((128, 256), BF16)
    zm = jnp.zeros((256, 256), F32)
    for e in range(8):
        pick = z_lane == e
        zm = zm + dot3(
            split(acts[:, e * 128 : (e + 1) * 128]),
            (jnp.where(pick, z_hi, zero), jnp.where(pick, z_lo, zero)),
        )
    imag_lane = (lane // 16) % 2 == 1
    swapped = jnp.where(imag_lane, pltpu.roll(zm, 16, 1), -pltpu.roll(zm, 240, 1))
    tag = jnp.maximum(tag_row, 0)
    pos = row % 128
    hot_x = jnp.where(pos == tag // 128, 1.0, 0.0).astype(BF16)
    hot_y = jnp.where(pos == tag % 128, 1.0, 0.0).astype(BF16)
    by_x = jnp.dot(xy[:512], hot_x, preferred_element_type=F32)
    by_y = jnp.dot(xy[512:], hot_y, preferred_element_type=F32)
    cos_x, sin_x, cos_y, sin_y = by_x[:256], by_x[256:], by_y[:256], by_y[256:]
    cos_part = cos_x * cos_y - sin_x * sin_y
    sin_part = -(sin_x * cos_y + cos_x * sin_y)
    out = dot3(split(cos_part), split(zm)) + dot3(split(sin_part), split(swapped))
    return out * (1.0 / math.sqrt(32768.0))


def modes_kernel(tag_col, tag_row, terms, z_hi, z_lo, xy, out):
    t = jnp.concatenate(
        [jnp.concatenate([terms[r, e] for r in range(8)], axis=0) for e in range(8)], axis=1
    )
    col = jnp.concatenate([tag_col[...]] * 2, axis=1)
    row = jnp.broadcast_to(tag_row[0:1, :], (256, 256))
    out[...] = modes_value(col, row, t, z_hi[...], z_lo[...], xy[...]).astype(out.dtype)


def kept_modes(tag_col, tag_row, terms):
    z_hi, z_lo, xy = (jnp.asarray(t) for t in tables())
    vm = pl.BlockSpec(memory_space=pltpu.VMEM)
    return pl.pallas_call(
        modes_kernel,
        out_shape=jax.ShapeDtypeStruct((256, 256), BF16),
        in_specs=[vm] * 6,
        out_specs=vm,
        compiler_params=pltpu.CompilerParams(vmem_limit_bytes=VMEM_BYTES),
        name="kept_modes",
    )(tag_col, tag_row, terms, z_hi, z_lo, xy)


def grad_kernel(x, g, out):
    sign = jnp.where(lax.broadcasted_iota(jnp.int32, (16, 128), 1) < 64, 1.0, -1.0)

    def mode_rows(k, carry):
        xk = x[k].astype(F32)
        rows = pl.ds(pl.multiple_of(k * 16, 16), 16)
        acc = [jnp.zeros((16, 128), F32) for _ in range(4)]
        for s in range(32):
            gs = g[s, rows, :].astype(F32)
            for q in range(4):
                acc[q] = acc[q] + xk[q * 16 : (q + 1) * 16, s : s + 1] * gs
        for i in range(2):
            out[i, rows, :] = acc[2 * i] + sign * pltpu.roll(acc[2 * i + 1], 64, 1)
        return carry

    lax.fori_loop(0, 32, mode_rows, 0)


def weight_grad(x, g):
    vm = pl.BlockSpec(memory_space=pltpu.VMEM)
    return pl.pallas_call(
        grad_kernel,
        out_shape=jax.ShapeDtypeStruct((2, 512, 128), F32),
        in_specs=[vm] * 2,
        out_specs=vm,
        compiler_params=pltpu.CompilerParams(vmem_limit_bytes=VMEM_BYTES),
        name="weight_grad",
    )(x, g)


def per_device(
    point_feats, point_coords, slot_block, slot_cell, slot_count, cotangent,
    offset_map, offset_bias, kernel_mix, lift_weight,
):
    grads = cotangent[0].reshape(512, 128).astype(BF16)
    grads_all = lax.all_gather(grads, "dp", axis=0, tiled=False)
    cells = slot_cell[0, 0]
    counts = slot_count[0, 0]
    is_live = jnp.arange(4, dtype=jnp.int32)[None, :] < counts[:, None]
    tags = jnp.where(is_live, jnp.arange(8, dtype=jnp.int32)[:, None] * 2048 + cells, -1).reshape(1, 32)
    tags_in = lax.all_to_all(jnp.broadcast_to(tags, (8, 32)), "slab", 0, 0, tiled=True).reshape(256)
    tag_col = jnp.broadcast_to(tags_in[:, None], (256, 128))
    tag_row = jnp.broadcast_to(tags_in[None, :], (8, 256))
    mix = jnp.transpose(kernel_mix, (0, 2, 1)).reshape(4096, 64)
    coef = jnp.concatenate([offset_map, offset_bias[:, None]], axis=1)
    terms = lifted_terms(
        slot_block.reshape(32), slot_cell.reshape(32), counts, offset_map.reshape(192),
        point_feats[0], point_coords[0], mix, coef, lift_weight.T,
    )
    terms_in = lax.all_to_all(terms, "slab", 0, 0, tiled=True)
    x = kept_modes(tag_col, tag_row, terms_in)
    x = lax.all_to_all(x.reshape(8, 32, 256), "slab", 0, 0, tiled=True)
    x = x.reshape(8, 32, 4, 64).transpose(0, 2, 1, 3).reshape(32, 32, 64)
    x = lax.all_to_all(x, "dp", 0, 0, tiled=True)
    grad = weight_grad(x.transpose(1, 2, 0), grads_all)
    return grad.reshape(2, 2, 16, 16, 128)


def solution(mesh):
    placed = (
        P("dp", "slab", None, None), P("dp", "slab", None, None), P("dp", "slab", None, None),
        P("dp", "slab", None, None), P("dp", "slab", None), P("dp", "slab", None, None, None),
        P(), P(), P(), P(),
    )
    return jax.shard_map(
        per_device,
        mesh=mesh,
        in_specs=placed,
        out_specs=P("dp", "slab", None, None, None),
        check_vma=False,
    )
```

```python
import math

import jax
import jax.numpy as jnp
import numpy as np
from jax import lax
from jax.experimental import pallas as pl
from jax.experimental.pallas import tpu as pltpu
from jax.sharding import PartitionSpec as P

F32 = jnp.float32
BF16 = jnp.bfloat16
NT = (((1,), (1,)), ((), ()))
VMEM_BYTES = 60 * 2**20


def split(x):
    hi = x.astype(BF16)
    return hi, (x - hi.astype(F32)).astype(BF16)


def dot3(a, b):
    ah, al = a
    bh, bl = b
    out = jnp.dot(ah, bh, preferred_element_type=F32)
    out = out + jnp.dot(al, bh, preferred_element_type=F32)
    return out + jnp.dot(ah, bl, preferred_element_type=F32)


def np_split(x):
    hi = np.asarray(x, np.float32).astype(BF16)
    lo = (np.asarray(x, np.float64) - hi.astype(np.float64)).astype(BF16)
    return hi, lo


def tables():
    z = np.arange(128)
    k = np.arange(16)
    turn = np.mod(z[:, None] * k[None, :], 128) * (2.0 * np.pi / 128)
    z_table = np.tile(np.concatenate([np.cos(turn), -np.sin(turn)], axis=1), (1, 8))
    z_hi, z_lo = np_split(z_table)
    signed = np.where(k < 8, k, k - 16)
    angle = np.mod(signed[:, None] * z[None, :], 128) * (2.0 * np.pi / 128)
    by_x = np.repeat(angle, 16, axis=0)
    by_y = np.tile(angle, (16, 1))
    xy = []
    for part in (np.cos(by_x), np.sin(by_x), np.cos(by_y), np.sin(by_y)):
        xy.append(np.concatenate(np_split(part), axis=1))
    return z_hi, z_lo, np.concatenate(xy, axis=0)


def terms_kernel(
    blk, cel, cnt, om, feats, coords, kmix, coef, bias_ref, lift_ref, cot,
    out, tags, cot_out, mixed, mix, tab, base, lifted, live, todo, seen,
):
    for b in range(16):
        seen[b] = 0

    def scan(n, carry):
        n_live, n_todo = carry
        slab = n // 4
        j = n - slab * 4
        is_live = j < cnt[slab]
        b = blk[slab, j]
        fresh = jnp.logical_and(is_live, seen[b] == 0)
        live[n_live] = n
        todo[n_todo] = b
        seen[b] = jnp.where(is_live, 1, seen[b])
        return n_live + is_live.astype(jnp.int32), n_todo + fresh.astype(jnp.int32)

    n_live, n_todo = lax.fori_loop(0, 32, scan, (jnp.int32(0), jnp.int32(0)))
    place = lax.broadcasted_iota(jnp.int32, (8, 256), 1) - 32 * lax.axis_index("slab")
    tag = jnp.zeros((8, 256), F32)
    for n in range(32):
        value = jnp.where(n % 4 < cnt[n // 4], (n // 4) * 2048 + cel[n // 4, n % 4], -1).astype(F32)
        tag = jnp.where(place == n, value, tag)
    tags[...] = tag
    for a in range(4):
        cot_out[a] = cot[a * 128 : (a + 1) * 128, :].T.astype(BF16)
    for h in range(32):
        both = jnp.concatenate([kmix[2 * h], kmix[2 * h + 1]], axis=1).astype(F32)
        mix[h * 128 : (h + 1) * 128, :] = both.T.astype(BF16)
    lifted[...] = jnp.zeros_like(lifted)
    pos_z = (lax.broadcasted_iota(jnp.int32, (128, 128), 0).astype(F32) + 0.5) * (1.0 / 128)

    def fill(h, carry):
        tab[h] = pos_z * om[h, 2]
        return carry

    lax.fori_loop(0, 64, fill, 0)

    def mix_pair(i, carry):
        b0 = todo[2 * i]
        b1 = todo[jnp.minimum(2 * i + 1, n_todo - 1)]
        pair = jnp.concatenate([feats[b0], feats[b1]], axis=1)

        def rows(r, carry):
            start = pl.multiple_of(r * 512, 512)
            m = jnp.dot(mix[pl.ds(start, 512), :], pair, preferred_element_type=F32).astype(BF16)
            mixed[b0, pl.ds(start, 512), :] = m[:, :128]
            mixed[b1, pl.ds(start, 512), :] = m[:, 128:]
            return carry

        return lax.fori_loop(0, 8, rows, carry)

    lax.fori_loop(0, (n_todo + 1) // 2, mix_pair, 0)
    coef_x, coef_y, coef_z = (coef[:, c : c + 1] for c in range(3))
    bias = bias_ref[...]
    lift_v = lift_ref[...].astype(F32).T.astype(BF16)

    def slot(i, carry):
        n = live[i]
        slab = n // 4
        b = blk[slab, n - slab * 4]
        cell = cel[slab, n - slab * 4]
        x = slab * 16 + cell // 128
        y = lax.rem(cell, 128)
        pos_x = (x.astype(F32) + 0.5) * (1.0 / 128)
        pos_y = (y.astype(F32) + 0.5) * (1.0 / 128)
        q = coords[b].astype(F32)
        point = coef_x * q[0:1] + coef_y * q[1:2] + coef_z * q[2:3]
        base[...] = (coef_x * pos_x + coef_y * pos_y) + bias - point
        ws, ms = [], []
        for h in range(64):
            w = (tab[h] + base[pl.ds(h, 1), :]).astype(BF16)
            ws.append(jnp.maximum(w, jnp.zeros_like(w)))
            ms.append(mixed[b, h * 64 : (h + 1) * 64, :])
        total = lax.dot_general(
            jnp.concatenate(ws, axis=1), jnp.concatenate(ms, axis=1), NT, preferred_element_type=F32
        )
        hi, lo = split(total.T * (1.0 / 128))
        pre = jnp.dot(lift_v, hi, preferred_element_type=F32) + jnp.dot(lift_v, lo, preferred_element_type=F32)
        lifted[pl.ds(pl.multiple_of(n * 64, 64), 64), :] = pre
        return carry

    lax.fori_loop(0, n_live, slot, 0)
    for e in range(64):
        out[e // 8, e % 8] = lifted[pl.ds(e, 32, stride=64), :].astype(BF16)


def lifted_terms(*args):
    sm = pl.BlockSpec(memory_space=pltpu.SMEM)
    vm = pl.BlockSpec(memory_space=pltpu.VMEM)
    return pl.pallas_call(
        terms_kernel,
        out_shape=(
            jax.ShapeDtypeStruct((8, 8, 32, 128), BF16),
            jax.ShapeDtypeStruct((8, 256), F32),
            jax.ShapeDtypeStruct((4, 128, 128), BF16),
        ),
        in_specs=[sm] * 4 + [vm] * 7,
        out_specs=(vm, vm, vm),
        scratch_shapes=[
            pltpu.VMEM((16, 4096, 128), BF16),
            pltpu.VMEM((4096, 64), BF16),
            pltpu.VMEM((64, 128, 128), F32),
            pltpu.VMEM((64, 128), F32),
            pltpu.VMEM((32 * 64, 128), F32),
            pltpu.SMEM((33,), jnp.int32),
            pltpu.SMEM((33,), jnp.int32),
            pltpu.SMEM((16,), jnp.int32),
        ],
        compiler_params=pltpu.CompilerParams(vmem_limit_bytes=VMEM_BYTES),
        name="slot_terms",
    )(*args)


def modes_value(tag_col, tag_row, terms, z_hi, z_lo, xy):
    lane = lax.broadcasted_iota(jnp.int32, (256, 256), 1)
    row = lax.broadcasted_iota(jnp.int32, (256, 256), 0)
    same = jnp.logical_and(tag_col == tag_row, tag_row >= 0)
    before = jnp.logical_and(same, lane < row)
    early = jnp.max(jnp.where(before, 1.0, 0.0), axis=1, keepdims=True)
    leader = jnp.where(tag_col[:, :1] >= 0, 1.0 - early, 0.0)
    sums = jnp.dot(jnp.where(same, 1.0, 0.0).astype(BF16), terms, preferred_element_type=F32)
    inner = math.sqrt(2.0 / math.pi) * (sums + 0.044715 * (sums * sums * sums))
    acts = (0.5 * leader) * (sums * (1.0 + jnp.tanh(inner)))
    z_lane = lax.broadcasted_iota(jnp.int32, (128, 256), 1) // 32
    zero = jnp.zeros((128, 256), BF16)
    zm = jnp.zeros((256, 256), F32)
    for e in range(8):
        pick = z_lane == e
        zm = zm + dot3(
            split(acts[:, e * 128 : (e + 1) * 128]),
            (jnp.where(pick, z_hi, zero), jnp.where(pick, z_lo, zero)),
        )
    imag_lane = (lane // 16) % 2 == 1
    swapped = jnp.where(imag_lane, pltpu.roll(zm, 16, 1), -pltpu.roll(zm, 240, 1))
    tag = jnp.maximum(tag_row, 0)
    pos = row % 128
    hot_x = jnp.where(pos == tag // 128, 1.0, 0.0).astype(BF16)
    hot_y = jnp.where(pos == tag % 128, 1.0, 0.0).astype(BF16)
    by_x = jnp.dot(xy[:512], hot_x, preferred_element_type=F32)
    by_y = jnp.dot(xy[512:], hot_y, preferred_element_type=F32)
    cos_x, sin_x, cos_y, sin_y = by_x[:256], by_x[256:], by_y[:256], by_y[256:]
    cos_part = cos_x * cos_y - sin_x * sin_y
    sin_part = -(sin_x * cos_y + cos_x * sin_y)
    out = dot3(split(cos_part), split(zm)) + dot3(split(sin_part), split(swapped))
    return out * (1.0 / math.sqrt(32768.0))


def swap_rows_runs(x):
    rows, lanes = x.shape
    row = lax.broadcasted_iota(jnp.int32, x.shape, 0) % 8
    run = (lax.broadcasted_iota(jnp.int32, x.shape, 1) % 128) // 16
    for step in (1, 2, 4):
        row_bit = (row // step) % 2
        run_bit = (run // step) % 2
        down = pltpu.roll(pltpu.roll(x, lanes - 16 * step, 1), step, 0)
        up = pltpu.roll(pltpu.roll(x, 16 * step, 1), rows - step, 0)
        x = jnp.where(row_bit == run_bit, x, jnp.where(row_bit == 1, down, up))
    return x


def exchange_kernel(
    terms, tags, cot, z_hi, z_lo, xy, out,
    terms_in, tags_in, cot_in, x_out, x_in, pick, g_out, g_in, fold,
    t_send, t_recv, n_send, n_recv, c_send, c_recv, x_send, x_recv, g_send, g_recv,
):
    dp = lax.axis_index("dp")
    slab = lax.axis_index("slab")
    z = dp // 4
    part = dp - z * 4

    def copy_to(src, dst, send, recv, dp_to, slab_to):
        return pltpu.make_async_remote_copy(
            src_ref=src, dst_ref=dst, send_sem=send, recv_sem=recv,
            device_id=(dp_to, slab_to), device_id_type=pl.DeviceIdType.MESH,
        )

    def terms_copy(to):
        return copy_to(terms.at[to], terms_in.at[slab], t_send.at[to], t_recv.at[slab], dp, to)

    def tags_copy(to):
        return copy_to(tags, tags_in.at[slab], n_send.at[to], n_recv.at[slab], dp, to)

    def cot_copy(to):
        return copy_to(cot.at[lax.rem(to, 4)], cot_in.at[dp], c_send.at[to], c_recv.at[dp], to, slab)

    def x_copy(to):
        rows = pl.ds(pl.multiple_of(to * 8, 8), 8)
        dp_to = slab * 4 + lax.rem(to, 4)
        return copy_to(x_out.at[:, rows], x_in.at[dp], x_send.at[to], x_recv.at[dp], dp_to, to // 4)

    def g_copy(to):
        return copy_to(g_out.at[to], g_in.at[part], g_send.at[to], g_recv.at[part], z * 4 + to, slab)

    own_x = slab * 4 + part
    own_terms = pltpu.make_async_copy(terms.at[slab], terms_in.at[slab], t_recv.at[slab])
    own_tags = pltpu.make_async_copy(tags, tags_in.at[slab], n_recv.at[slab])
    own_cot = pltpu.make_async_copy(cot.at[part], cot_in.at[dp], c_recv.at[dp])
    own_rows = pl.ds(pl.multiple_of(own_x * 8, 8), 8)
    own_x_copy = pltpu.make_async_copy(x_out.at[:, own_rows], x_in.at[dp], x_recv.at[dp])
    to_self = z == slab

    def others(count, me, act):
        def step(i, carry):
            act(lax.rem(me + i, count))
            return carry

        lax.fori_loop(1, count, step, 0)

    barrier = pltpu.get_barrier_semaphore()

    def greet(dp_to, slab_to):
        pl.semaphore_signal(
            barrier, inc=1, device_id=(dp_to, slab_to), device_id_type=pl.DeviceIdType.MESH
        )

    others(8, slab, lambda to: greet(dp, to))
    others(32, dp, lambda to: greet(to, slab))
    others(32, dp, lambda to: greet(to, z))

    @pl.when(jnp.logical_not(to_self))
    def _():
        greet(dp, z)

    pl.semaphore_wait(barrier, 7 + 31 + 32 - to_self.astype(jnp.int32))

    own_terms.start()
    own_tags.start()
    own_cot.start()

    def start_slab(to):
        terms_copy(to).start()
        tags_copy(to).start()

    others(8, slab, start_slab)
    others(32, dp, lambda to: cot_copy(to).start())

    own_terms.wait()
    own_tags.wait()

    def wait_slab(frm):
        copy_to(terms.at[frm], terms_in.at[frm], t_send.at[frm], t_recv.at[frm], dp, frm).wait_recv()
        copy_to(tags, tags_in.at[frm], n_send.at[frm], n_recv.at[frm], dp, frm).wait_recv()

    others(8, slab, wait_slab)
    t = jnp.concatenate(
        [jnp.concatenate([terms_in[r, e] for r in range(8)], axis=0) for e in range(8)], axis=1
    )
    tag_sum = tags_in[0]
    for r in range(1, 8):
        tag_sum = tag_sum + tags_in[r]
    row = jnp.broadcast_to(tag_sum[0:1, :], (256, 256))
    x = modes_value(row.T.astype(jnp.int32), row.astype(jnp.int32), t, z_hi[...], z_lo[...], xy[...])
    x = swap_rows_runs(x)
    x_out[0] = x[:, :128]
    x_out[1] = x[:, 128:]

    @pl.when(to_self)
    def _():
        own_x_copy.start()

    @pl.when(jnp.logical_not(to_self))
    def _():
        x_copy(own_x).start()

    others(32, own_x, lambda to: x_copy(to).start())
    own_cot.wait()

    def wait_cot(frm):
        copy_to(cot.at[0], cot_in.at[frm], c_send.at[frm], c_recv.at[frm], frm, slab).wait_recv()

    others(32, dp, wait_cot)

    def wait_x(frm):
        copy_to(x_out.at[:, pl.ds(0, 8)], x_in.at[frm], x_send.at[frm], x_recv.at[frm], frm, z).wait_recv()

    others(32, dp, wait_x)

    @pl.when(to_self)
    def _():
        own_x_copy.wait()

    @pl.when(jnp.logical_not(to_self))
    def _():
        wait_x(dp)

    def channels(to):
        both = x_in[:, to // 2]
        pick[...] = jnp.where(lax.rem(to, 2) == 1, pltpu.roll(both, 4, 1), both)
        for o in range(4):
            low = pl.ds(o * 16, 16)
            high = pl.ds(64 + o * 16, 16)

            def sample(s, acc):
                g_low = cot_in[s, low, :].astype(F32)
                g_high = cot_in[s, high, :].astype(F32)
                new = []
                for q in range(4):
                    xq = pick[s, q : q + 1, :]
                    new.append(acc[2 * q] + xq * g_low)
                    new.append(acc[2 * q + 1] + xq * g_high)
                return tuple(new)

            acc = lax.fori_loop(0, 32, sample, tuple(jnp.zeros((16, 128), F32) for _ in range(8)), unroll=4)
            for i in range(2):
                re_low, re_high, im_low, im_high = acc[4 * i : 4 * i + 4]
                fold[i, low, :] = re_low + im_high
                fold[i, high, :] = re_high - im_low
        for i in range(2):
            g_out[to, i] = fold[i].T.astype(BF16)

    def one(k, carry):
        other = (1 - part // 2) * 2 + k
        here = (part // 2) * 2 + lax.rem(part + k + 1, 2)
        to = jnp.where(k < 2, other, here)
        channels(to)

        @pl.when(k < 3)
        def _():
            g_copy(to).start()

        return carry

    lax.fori_loop(0, 4, one, 0)
    out[0, part] = g_out[part, 0]
    out[1, part] = g_out[part, 1]

    def take(frm):
        copy_to(g_out.at[frm], g_in.at[frm], g_send.at[frm], g_recv.at[frm], z * 4 + frm, slab).wait_recv()
        out[0, frm] = g_in[frm, 0]
        out[1, frm] = g_in[frm, 1]

    others(4, part, take)

    def sent_slab(to):
        terms_copy(to).wait_send()
        tags_copy(to).wait_send()

    others(8, slab, sent_slab)
    others(32, dp, lambda to: cot_copy(to).wait_send())
    others(32, own_x, lambda to: x_copy(to).wait_send())

    @pl.when(jnp.logical_not(to_self))
    def _():
        x_copy(own_x).wait_send()

    others(4, part, lambda to: g_copy(to).wait_send())


def exchange(terms, tags, cot):
    z_hi, z_lo, xy = (jnp.asarray(t) for t in tables())
    vm = pl.BlockSpec(memory_space=pltpu.VMEM)
    dma = pltpu.SemaphoreType.DMA
    return pl.pallas_call(
        exchange_kernel,
        out_shape=jax.ShapeDtypeStruct((2, 4, 128, 128), BF16),
        in_specs=[vm] * 6,
        out_specs=vm,
        scratch_shapes=[
            pltpu.VMEM((8, 8, 32, 128), BF16),
            pltpu.VMEM((8, 8, 256), F32),
            pltpu.VMEM((32, 128, 128), BF16),
            pltpu.VMEM((2, 256, 128), F32),
            pltpu.VMEM((32, 2, 8, 128), F32),
            pltpu.VMEM((32, 8, 128), F32),
            pltpu.VMEM((4, 2, 128, 128), BF16),
            pltpu.VMEM((4, 2, 128, 128), BF16),
            pltpu.VMEM((2, 128, 128), F32),
            dma((8,)), dma((8,)), dma((8,)), dma((8,)), dma((32,)), dma((32,)),
            dma((32,)), dma((32,)), dma((4,)), dma((4,)),
        ],
        compiler_params=pltpu.CompilerParams(
            vmem_limit_bytes=VMEM_BYTES, collective_id=0, has_side_effects=True
        ),
        name="exchange",
    )(terms, tags, cot, z_hi, z_lo, xy)


def per_device(
    point_feats, point_coords, slot_block, slot_cell, slot_count, cotangent,
    offset_map, offset_bias, kernel_mix, lift_weight,
):
    terms, tags, cot = lifted_terms(
        slot_block[0, 0], slot_cell[0, 0], slot_count[0, 0], offset_map,
        point_feats[0], point_coords[0], kernel_mix, offset_map, offset_bias[:, None], lift_weight,
        cotangent.reshape(512, 128),
    )
    grad = exchange(terms, tags, cot)
    return grad.astype(F32).reshape(2, 2, 16, 16, 128)


def solution(mesh):
    placed = (
        P("dp", "slab", None, None), P("dp", "slab", None, None), P("dp", "slab", None, None),
        P("dp", "slab", None, None), P("dp", "slab", None), P("dp", "slab", None, None, None),
        P(), P(), P(), P(),
    )
    return jax.shard_map(
        per_device,
        mesh=mesh,
        in_specs=placed,
        out_specs=P("dp", "slab", None, None, None),
        check_vma=False,
    )
```

```python
import math

import jax
import jax.numpy as jnp
import numpy as np
from jax import lax
from jax.experimental import pallas as pl
from jax.experimental.pallas import tpu as pltpu
from jax.sharding import PartitionSpec as P

F32 = jnp.float32
BF16 = jnp.bfloat16
NT = (((1,), (1,)), ((), ()))
VMEM_BYTES = 60 * 2**20


def split(x):
    hi = x.astype(BF16)
    return hi, (x - hi.astype(F32)).astype(BF16)


def dot3(a, b):
    ah, al = a
    bh, bl = b
    out = jnp.dot(ah, bh, preferred_element_type=F32)
    out = out + jnp.dot(al, bh, preferred_element_type=F32)
    return out + jnp.dot(ah, bl, preferred_element_type=F32)


def np_split(x):
    hi = np.asarray(x, np.float32).astype(BF16)
    lo = (np.asarray(x, np.float64) - hi.astype(np.float64)).astype(BF16)
    return hi, lo


def tables():
    z = np.arange(128)
    k = np.arange(16)
    turn = np.mod(z[:, None] * k[None, :], 128) * (2.0 * np.pi / 128)
    z_table = np.tile(np.concatenate([np.cos(turn), -np.sin(turn)], axis=1), (1, 8))
    z_hi, z_lo = np_split(z_table)
    signed = np.where(k < 8, k, k - 16)
    angle = np.mod(signed[:, None] * z[None, :], 128) * (2.0 * np.pi / 128)
    by_x = np.repeat(angle, 16, axis=0)
    by_y = np.tile(angle, (16, 1))
    xy = []
    for part in (np.cos(by_x), np.sin(by_x), np.cos(by_y), np.sin(by_y)):
        xy.append(np.concatenate(np_split(part), axis=1))
    return z_hi, z_lo, np.concatenate(xy, axis=0)


def terms_kernel(
    blk, cel, cnt, om, feats, coords, kmix, coef_ref, bias_ref, lift_ref, cot,
    out, tags, cot_out, mixed, mix, tab, base, coef, points, lifted, live, todo, seen,
):
    for b in range(16):
        seen[b] = 0

    def scan(n, carry):
        n_live, n_todo = carry
        slab = n // 4
        j = n - slab * 4
        is_live = j < cnt[0, slab]
        b = blk[j, slab]
        fresh = jnp.logical_and(is_live, seen[b] == 0)
        live[n_live] = n
        todo[n_todo] = b
        seen[b] = jnp.where(is_live, 1, seen[b])
        return n_live + is_live.astype(jnp.int32), n_todo + fresh.astype(jnp.int32)

    n_live, n_todo = lax.fori_loop(0, 32, scan, (jnp.int32(0), jnp.int32(0)))
    place = lax.broadcasted_iota(jnp.int32, (8, 256), 1) - 32 * lax.axis_index("slab")
    tag = jnp.zeros((8, 256), F32)
    for n in range(32):
        value = jnp.where(n % 4 < cnt[0, n // 4], (n // 4) * 2048 + cel[n % 4, n // 4], -1).astype(F32)
        tag = jnp.where(place == n, value, tag)
    tags[...] = tag
    for a in range(4):
        cot_out[a] = cot[a * 128 : (a + 1) * 128, :].T.astype(BF16)
    for h in range(32):
        both = jnp.concatenate([kmix[2 * h], kmix[2 * h + 1]], axis=1).astype(F32)
        mix[h * 128 : (h + 1) * 128, :] = both.T.astype(BF16)
    lifted[...] = jnp.zeros_like(lifted)
    pos_z = (lax.broadcasted_iota(jnp.int32, (128, 128), 0).astype(F32) + 0.5) * (1.0 / 128)

    def fill(h, carry):
        tab[h] = pos_z * om[2, h]
        return carry

    lax.fori_loop(0, 64, fill, 0)

    def mix_pair(i, carry):
        b0 = todo[2 * i]
        b1 = todo[jnp.minimum(2 * i + 1, n_todo - 1)]
        pair = jnp.concatenate([feats[b0], feats[b1]], axis=1)

        def rows(r, carry):
            start = pl.multiple_of(r * 512, 512)
            m = jnp.dot(mix[pl.ds(start, 512), :], pair, preferred_element_type=F32).astype(BF16)
            mixed[b0, pl.ds(start, 512), :] = m[:, :128]
            mixed[b1, pl.ds(start, 512), :] = m[:, 128:]
            return carry

        return lax.fori_loop(0, 8, rows, carry)

    lax.fori_loop(0, (n_todo + 1) // 2, mix_pair, 0)
    for c in range(3):
        coef[c] = jnp.broadcast_to(coef_ref[c : c + 1, :], (128, 64)).T
    coef[3] = jnp.broadcast_to(bias_ref[...], (128, 64)).T
    for c in range(3):
        by_block = coords[c].astype(F32)
        for b in range(16):
            points[b, c : c + 1, :] = by_block[b : b + 1, :]
    lift_v = lift_ref[...].astype(F32).T.astype(BF16)

    def slot(i, carry):
        n = live[i]
        slab = n // 4
        b = blk[n - slab * 4, slab]
        cell = cel[n - slab * 4, slab]
        x = slab * 16 + cell // 128
        y = lax.rem(cell, 128)
        pos_x = (x.astype(F32) + 0.5) * (1.0 / 128)
        pos_y = (y.astype(F32) + 0.5) * (1.0 / 128)
        coef_x, coef_y, coef_z = coef[0], coef[1], coef[2]
        point = coef_x * points[b, 0:1] + coef_y * points[b, 1:2] + coef_z * points[b, 2:3]
        base[...] = (coef_x * pos_x + coef_y * pos_y) + coef[3] - point
        ws, ms = [], []
        for h in range(64):
            w = (tab[h] + base[pl.ds(h, 1), :]).astype(BF16)
            ws.append(jnp.maximum(w, jnp.zeros_like(w)))
            ms.append(mixed[b, h * 64 : (h + 1) * 64, :])
        half = 32
        by_z = lax.dot_general(
            jnp.concatenate(ws[:half], axis=1), jnp.concatenate(ms[:half], axis=1), NT, preferred_element_type=F32
        )
        by_d = lax.dot_general(
            jnp.concatenate(ms[half:], axis=1), jnp.concatenate(ws[half:], axis=1), NT, preferred_element_type=F32
        )
        hi, lo = split((by_z.T + by_d) * (1.0 / 128))
        pre = jnp.dot(lift_v, hi, preferred_element_type=F32) + jnp.dot(lift_v, lo, preferred_element_type=F32)
        lifted[pl.ds(pl.multiple_of(n * 64, 64), 64), :] = pre
        return carry

    lax.fori_loop(0, n_live, slot, 0)
    for e in range(64):
        out[e // 8, e % 8] = lifted[pl.ds(e, 32, stride=64), :].astype(BF16)


def lifted_terms(*args):
    sm = pl.BlockSpec(memory_space=pltpu.SMEM)
    vm = pl.BlockSpec(memory_space=pltpu.VMEM)
    return pl.pallas_call(
        terms_kernel,
        out_shape=(
            jax.ShapeDtypeStruct((8, 8, 32, 128), BF16),
            jax.ShapeDtypeStruct((8, 256), F32),
            jax.ShapeDtypeStruct((4, 128, 128), BF16),
        ),
        in_specs=[sm] * 4 + [vm] * 7,
        out_specs=(vm, vm, vm),
        scratch_shapes=[
            pltpu.VMEM((16, 4096, 128), BF16),
            pltpu.VMEM((4096, 64), BF16),
            pltpu.VMEM((64, 128, 128), F32),
            pltpu.VMEM((64, 128), F32),
            pltpu.VMEM((4, 64, 128), F32),
            pltpu.VMEM((16, 8, 128), F32),
            pltpu.VMEM((32 * 64, 128), F32),
            pltpu.SMEM((33,), jnp.int32),
            pltpu.SMEM((33,), jnp.int32),
            pltpu.SMEM((16,), jnp.int32),
        ],
        compiler_params=pltpu.CompilerParams(vmem_limit_bytes=VMEM_BYTES),
        name="slot_terms",
    )(*args)


def modes_value(tag_col, tag_row, terms, z_hi, z_lo, xy):
    lane = lax.broadcasted_iota(jnp.int32, (256, 256), 1)
    row = lax.broadcasted_iota(jnp.int32, (256, 256), 0)
    same = jnp.logical_and(tag_col == tag_row, tag_row >= 0)
    before = jnp.logical_and(same, lane < row)
    early = jnp.max(jnp.where(before, 1.0, 0.0), axis=1, keepdims=True)
    leader = jnp.where(tag_col[:, :1] >= 0, 1.0 - early, 0.0)
    sums = jnp.dot(jnp.where(same, 1.0, 0.0).astype(BF16), terms, preferred_element_type=F32)
    inner = math.sqrt(2.0 / math.pi) * (sums + 0.044715 * (sums * sums * sums))
    acts = (0.5 * leader) * (sums * (1.0 + jnp.tanh(inner)))
    z_lane = lax.broadcasted_iota(jnp.int32, (128, 256), 1) // 32
    zero = jnp.zeros((128, 256), BF16)
    zm = jnp.zeros((256, 256), F32)
    for e in range(8):
        pick = z_lane == e
        zm = zm + dot3(
            split(acts[:, e * 128 : (e + 1) * 128]),
            (jnp.where(pick, z_hi, zero), jnp.where(pick, z_lo, zero)),
        )
    imag_lane = (lane // 16) % 2 == 1
    swapped = jnp.where(imag_lane, pltpu.roll(zm, 16, 1), -pltpu.roll(zm, 240, 1))
    tag = jnp.maximum(tag_row, 0)
    pos = row % 128
    hot_x = jnp.where(pos == tag // 128, 1.0, 0.0).astype(BF16)
    hot_y = jnp.where(pos == tag % 128, 1.0, 0.0).astype(BF16)
    by_x = jnp.dot(xy[:512], hot_x, preferred_element_type=F32)
    by_y = jnp.dot(xy[512:], hot_y, preferred_element_type=F32)
    cos_x, sin_x, cos_y, sin_y = by_x[:256], by_x[256:], by_y[:256], by_y[256:]
    cos_part = cos_x * cos_y - sin_x * sin_y
    sin_part = -(sin_x * cos_y + cos_x * sin_y)
    out = dot3(split(cos_part), split(zm)) + dot3(split(sin_part), split(swapped))
    return out * (1.0 / math.sqrt(32768.0))


def swap_rows_runs(x):
    rows, lanes = x.shape
    row = lax.broadcasted_iota(jnp.int32, x.shape, 0) % 8
    run = (lax.broadcasted_iota(jnp.int32, x.shape, 1) % 128) // 16
    for step in (1, 2, 4):
        row_bit = (row // step) % 2
        run_bit = (run // step) % 2
        down = pltpu.roll(pltpu.roll(x, lanes - 16 * step, 1), step, 0)
        up = pltpu.roll(pltpu.roll(x, 16 * step, 1), rows - step, 0)
        x = jnp.where(row_bit == run_bit, x, jnp.where(row_bit == 1, down, up))
    return x


def exchange_kernel(
    terms, tags, cot, z_hi, z_lo, xy, out,
    terms_in, tags_in, cot_in, x_out, x_mid, x_in, pick, g_out, g_in, fold,
    t_send, t_recv, n_send, n_recv, c_send, c_recv, y_send, y_recv, x_send, x_recv, g_send, g_recv,
):
    dp = lax.axis_index("dp")
    slab = lax.axis_index("slab")
    z = dp // 4
    part = dp - z * 4

    def copy_to(src, dst, send, recv, dp_to, slab_to):
        return pltpu.make_async_remote_copy(
            src_ref=src, dst_ref=dst, send_sem=send, recv_sem=recv,
            device_id=(dp_to, slab_to), device_id_type=pl.DeviceIdType.MESH,
        )

    def terms_copy(to):
        return copy_to(terms.at[to], terms_in.at[slab], t_send.at[to], t_recv.at[slab], dp, to)

    def tags_copy(to):
        return copy_to(tags, tags_in.at[slab], n_send.at[to], n_recv.at[slab], dp, to)

    def cot_copy(to):
        return copy_to(cot.at[lax.rem(to, 4)], cot_in.at[dp], c_send.at[to], c_recv.at[dp], to, slab)

    def slab_rows(at):
        return x_out.at[:, pl.ds(pl.multiple_of(at * 32, 32), 32)]

    def part_rows(at):
        return x_mid.at[at // 4, :, pl.ds(pl.multiple_of(lax.rem(at, 4) * 8, 8), 8)]

    def y_copy(to):
        return copy_to(slab_rows(to), x_mid.at[slab], y_send.at[to], y_recv.at[slab], dp, to)

    def x_copy(to):
        return copy_to(part_rows(to), x_in.at[dp], x_send.at[to], x_recv.at[dp], to, slab)

    def g_copy(to):
        return copy_to(g_out.at[to], g_in.at[part], g_send.at[to], g_recv.at[part], z * 4 + to, slab)

    own_terms = pltpu.make_async_copy(terms.at[slab], terms_in.at[slab], t_recv.at[slab])
    own_tags = pltpu.make_async_copy(tags, tags_in.at[slab], n_recv.at[slab])
    own_cot = pltpu.make_async_copy(cot.at[part], cot_in.at[dp], c_recv.at[dp])
    own_y = pltpu.make_async_copy(slab_rows(slab), x_mid.at[slab], y_recv.at[slab])
    own_x = pltpu.make_async_copy(part_rows(dp), x_in.at[dp], x_recv.at[dp])

    def others(count, me, act):
        def step(i, carry):
            act(lax.rem(me + i, count))
            return carry

        lax.fori_loop(1, count, step, 0)

    barrier = pltpu.get_barrier_semaphore()

    def greet(dp_to, slab_to):
        pl.semaphore_signal(
            barrier, inc=1, device_id=(dp_to, slab_to), device_id_type=pl.DeviceIdType.MESH
        )

    others(8, slab, lambda to: greet(dp, to))
    others(32, dp, lambda to: greet(to, slab))
    pl.semaphore_wait(barrier, 7 + 31)

    own_terms.start()
    own_tags.start()
    own_cot.start()

    def start_slab(to):
        terms_copy(to).start()
        tags_copy(to).start()

    others(8, slab, start_slab)
    others(32, dp, lambda to: cot_copy(to).start())

    own_terms.wait()
    own_tags.wait()

    def wait_slab(frm):
        copy_to(terms.at[frm], terms_in.at[frm], t_send.at[frm], t_recv.at[frm], dp, frm).wait_recv()
        copy_to(tags, tags_in.at[frm], n_send.at[frm], n_recv.at[frm], dp, frm).wait_recv()

    others(8, slab, wait_slab)
    t = jnp.concatenate(
        [jnp.concatenate([terms_in[r, e] for r in range(8)], axis=0) for e in range(8)], axis=1
    )
    tag_sum = tags_in[0]
    for r in range(1, 8):
        tag_sum = tag_sum + tags_in[r]
    row = jnp.broadcast_to(tag_sum[0:1, :], (256, 256))
    x = modes_value(row.T.astype(jnp.int32), row.astype(jnp.int32), t, z_hi[...], z_lo[...], xy[...])
    x = swap_rows_runs(x)
    x_out[0] = x[:, :128]
    x_out[1] = x[:, 128:]

    own_y.start()
    others(8, slab, lambda to: y_copy(to).start())

    def pass_on(frm):
        for a in range(4):
            to = frm * 4 + a

            @pl.when(to == dp)
            def _():
                own_x.start()

            @pl.when(to != dp)
            def _():
                x_copy(to).start()

    own_y.wait()
    pass_on(slab)

    def relay(frm):
        copy_to(slab_rows(0), x_mid.at[frm], y_send.at[frm], y_recv.at[frm], dp, frm).wait_recv()
        pass_on(frm)

    others(8, slab, relay)
    own_cot.wait()

    def wait_cot(frm):
        copy_to(cot.at[0], cot_in.at[frm], c_send.at[frm], c_recv.at[frm], frm, slab).wait_recv()

    others(32, dp, wait_cot)

    def wait_x(frm):
        copy_to(part_rows(0), x_in.at[frm], x_send.at[frm], x_recv.at[frm], frm, slab).wait_recv()

    own_x.wait()
    others(32, dp, wait_x)

    def channels(to):
        both = x_in[:, to // 2]
        pick[...] = jnp.where(lax.rem(to, 2) == 1, pltpu.roll(both, 4, 1), both)
        for o in range(4):
            low = pl.ds(o * 16, 16)
            high = pl.ds(64 + o * 16, 16)

            def sample(s, acc):
                g_low = cot_in[s, low, :].astype(F32)
                g_high = cot_in[s, high, :].astype(F32)
                new = []
                for q in range(4):
                    xq = pick[s, q : q + 1, :]
                    new.append(acc[2 * q] + xq * g_low)
                    new.append(acc[2 * q + 1] + xq * g_high)
                return tuple(new)

            acc = lax.fori_loop(0, 32, sample, tuple(jnp.zeros((16, 128), F32) for _ in range(8)), unroll=4)
            for i in range(2):
                re_low, re_high, im_low, im_high = acc[4 * i : 4 * i + 4]
                fold[i, low, :] = re_low + im_high
                fold[i, high, :] = re_high - im_low
        for i in range(2):
            g_out[to, i] = fold[i].T.astype(BF16)

    def one(k, carry):
        other = (1 - part // 2) * 2 + k
        here = (part // 2) * 2 + lax.rem(part + k + 1, 2)
        to = jnp.where(k < 2, other, here)
        channels(to)

        @pl.when(k < 3)
        def _():
            g_copy(to).start()

        return carry

    lax.fori_loop(0, 4, one, 0)
    out[0, part] = g_out[part, 0]
    out[1, part] = g_out[part, 1]

    def take(frm):
        copy_to(g_out.at[frm], g_in.at[frm], g_send.at[frm], g_recv.at[frm], z * 4 + frm, slab).wait_recv()
        out[0, frm] = g_in[frm, 0]
        out[1, frm] = g_in[frm, 1]

    others(4, part, take)

    def sent_slab(to):
        terms_copy(to).wait_send()
        tags_copy(to).wait_send()

    others(8, slab, sent_slab)
    others(32, dp, lambda to: cot_copy(to).wait_send())
    others(8, slab, lambda to: y_copy(to).wait_send())
    others(32, dp, lambda to: x_copy(to).wait_send())
    others(4, part, lambda to: g_copy(to).wait_send())


def exchange(terms, tags, cot):
    z_hi, z_lo, xy = (jnp.asarray(t) for t in tables())
    vm = pl.BlockSpec(memory_space=pltpu.VMEM)
    dma = pltpu.SemaphoreType.DMA
    return pl.pallas_call(
        exchange_kernel,
        out_shape=jax.ShapeDtypeStruct((2, 4, 128, 128), BF16),
        in_specs=[vm] * 6,
        out_specs=vm,
        scratch_shapes=[
            pltpu.VMEM((8, 8, 32, 128), BF16),
            pltpu.VMEM((8, 8, 256), F32),
            pltpu.VMEM((32, 128, 128), BF16),
            pltpu.VMEM((2, 256, 128), F32),
            pltpu.VMEM((8, 2, 32, 128), F32),
            pltpu.VMEM((32, 2, 8, 128), F32),
            pltpu.VMEM((32, 8, 128), F32),
            pltpu.VMEM((4, 2, 128, 128), BF16),
            pltpu.VMEM((4, 2, 128, 128), BF16),
            pltpu.VMEM((2, 128, 128), F32),
            dma((8,)), dma((8,)), dma((8,)), dma((8,)), dma((32,)), dma((32,)),
            dma((8,)), dma((8,)), dma((32,)), dma((32,)), dma((4,)), dma((4,)),
        ],
        compiler_params=pltpu.CompilerParams(
            vmem_limit_bytes=VMEM_BYTES, collective_id=0, has_side_effects=True
        ),
        name="exchange",
    )(terms, tags, cot, z_hi, z_lo, xy)


def per_device(
    point_feats, point_coords, slot_block, slot_cell, slot_count, cotangent,
    offset_map, offset_bias, kernel_mix, lift_weight,
):
    terms, tags, cot = lifted_terms(
        slot_block[0, 0].T, slot_cell[0, 0].T, slot_count[0], offset_map.T,
        point_feats[0], point_coords[0].transpose(1, 0, 2), kernel_mix, offset_map.T, offset_bias[None, :], lift_weight,
        cotangent.reshape(512, 128),
    )
    grad = exchange(terms, tags, cot)
    return grad.astype(F32).reshape(2, 2, 16, 16, 128)


def solution(mesh):
    placed = (
        P("dp", "slab", None, None), P("dp", "slab", None, None), P("dp", "slab", None, None),
        P("dp", "slab", None, None), P("dp", "slab", None), P("dp", "slab", None, None, None),
        P(), P(), P(), P(),
    )
    return jax.shard_map(
        per_device,
        mesh=mesh,
        in_specs=placed,
        out_specs=P("dp", "slab", None, None, None),
        check_vma=False,
    )
```

```python
import math

import jax
import jax.numpy as jnp
import numpy as np
from jax import lax
from jax.experimental import pallas as pl
from jax.experimental.pallas import tpu as pltpu
from jax.sharding import PartitionSpec as P

F32 = jnp.float32
BF16 = jnp.bfloat16
NT = (((1,), (1,)), ((), ()))
VMEM_BYTES = 60 * 2**20


def split(x):
    hi = x.astype(BF16)
    return hi, (x - hi.astype(F32)).astype(BF16)


def dot3(a, b):
    ah, al = a
    bh, bl = b
    out = jnp.dot(ah, bh, preferred_element_type=F32)
    out = out + jnp.dot(al, bh, preferred_element_type=F32)
    return out + jnp.dot(ah, bl, preferred_element_type=F32)


def np_split(x):
    hi = np.asarray(x, np.float32).astype(BF16)
    lo = (np.asarray(x, np.float64) - hi.astype(np.float64)).astype(BF16)
    return hi, lo


def tables():
    z = np.arange(128)
    k = np.arange(16)
    turn = np.mod(z[:, None] * k[None, :], 128) * (2.0 * np.pi / 128)
    z_table = np.tile(np.concatenate([np.cos(turn), -np.sin(turn)], axis=1), (1, 8))
    z_hi, z_lo = np_split(z_table)
    signed = np.where(k < 8, k, k - 16)
    angle = np.mod(signed[:, None] * z[None, :], 128) * (2.0 * np.pi / 128)
    by_x = np.repeat(angle, 16, axis=0)
    by_y = np.tile(angle, (16, 1))
    xy = []
    for part in (np.cos(by_x), np.sin(by_x), np.cos(by_y), np.sin(by_y)):
        xy.append(np.concatenate(np_split(part), axis=1))
    return z_hi, z_lo, np.concatenate(xy, axis=0)


def terms_kernel(
    blk, cel, cnt, om, feats, coords, kmix, coef_ref, bias_ref, lift_ref, cot,
    out, tags, cot_out, mixed, mix, tab, base, coef, points, lifted, live, todo, seen,
):
    for b in range(16):
        seen[b] = 0

    def scan(n, carry):
        n_live, n_todo = carry
        slab = n // 4
        j = n - slab * 4
        is_live = j < cnt[0, slab]
        b = blk[j, slab]
        fresh = jnp.logical_and(is_live, seen[b] == 0)
        live[n_live] = n
        todo[n_todo] = b
        seen[b] = jnp.where(is_live, 1, seen[b])
        return n_live + is_live.astype(jnp.int32), n_todo + fresh.astype(jnp.int32)

    n_live, n_todo = lax.fori_loop(0, 32, scan, (jnp.int32(0), jnp.int32(0)))
    place = lax.broadcasted_iota(jnp.int32, (8, 256), 1) - 32 * lax.axis_index("slab")
    tag = jnp.zeros((8, 256), F32)
    for n in range(32):
        value = jnp.where(n % 4 < cnt[0, n // 4], (n // 4) * 2048 + cel[n % 4, n // 4], -1).astype(F32)
        tag = jnp.where(place == n, value, tag)
    tags[...] = tag
    for a in range(4):
        cot_out[a] = cot[a * 128 : (a + 1) * 128, :].T.astype(BF16)
    for h in range(32):
        both = jnp.concatenate([kmix[2 * h], kmix[2 * h + 1]], axis=1).astype(F32)
        mix[h * 128 : (h + 1) * 128, :] = both.T.astype(BF16)
    lifted[...] = jnp.zeros_like(lifted)
    pos_z = (lax.broadcasted_iota(jnp.int32, (128, 128), 0).astype(F32) + 0.5) * (1.0 / 128)

    def fill(h, carry):
        tab[h] = pos_z * om[2, h]
        return carry

    lax.fori_loop(0, 64, fill, 0)

    def mix_pair(i, carry):
        b0 = todo[2 * i]
        b1 = todo[jnp.minimum(2 * i + 1, n_todo - 1)]
        pair = jnp.concatenate([feats[b0], feats[b1]], axis=1)

        def rows(r, carry):
            start = pl.multiple_of(r * 512, 512)
            m = jnp.dot(mix[pl.ds(start, 512), :], pair, preferred_element_type=F32).astype(BF16)
            mixed[b0, pl.ds(start, 512), :] = m[:, :128]
            mixed[b1, pl.ds(start, 512), :] = m[:, 128:]
            return carry

        return lax.fori_loop(0, 8, rows, carry)

    lax.fori_loop(0, (n_todo + 1) // 2, mix_pair, 0)
    for c in range(3):
        coef[c] = jnp.broadcast_to(coef_ref[c : c + 1, :], (128, 64)).T
    coef[3] = jnp.broadcast_to(bias_ref[...], (128, 64)).T
    for c in range(3):
        by_block = coords[c].astype(F32)
        for b in range(16):
            points[b, c : c + 1, :] = by_block[b : b + 1, :]
    lift_v = lift_ref[...].astype(F32).T.astype(BF16)

    def slot(i, carry):
        n = live[i]
        slab = n // 4
        b = blk[n - slab * 4, slab]
        cell = cel[n - slab * 4, slab]
        x = slab * 16 + cell // 128
        y = lax.rem(cell, 128)
        pos_x = (x.astype(F32) + 0.5) * (1.0 / 128)
        pos_y = (y.astype(F32) + 0.5) * (1.0 / 128)
        coef_x, coef_y, coef_z = coef[0], coef[1], coef[2]
        point = coef_x * points[b, 0:1] + coef_y * points[b, 1:2] + coef_z * points[b, 2:3]
        base[...] = (coef_x * pos_x + coef_y * pos_y) + coef[3] - point
        ws, ms = [], []
        for h in range(64):
            w = (tab[h] + base[pl.ds(h, 1), :]).astype(BF16)
            ws.append(jnp.maximum(w, jnp.zeros_like(w)))
            ms.append(mixed[b, h * 64 : (h + 1) * 64, :])
        total = lax.dot_general(
            jnp.concatenate(ws, axis=1), jnp.concatenate(ms, axis=1), NT, preferred_element_type=F32
        )
        hi, lo = split(total.T * (1.0 / 128))
        pre = jnp.dot(lift_v, hi, preferred_element_type=F32) + jnp.dot(lift_v, lo, preferred_element_type=F32)
        lifted[pl.ds(pl.multiple_of(n * 64, 64), 64), :] = pre
        return carry

    lax.fori_loop(0, n_live, slot, 0)
    for e in range(64):
        out[e // 8, e % 8] = lifted[pl.ds(e, 32, stride=64), :].astype(BF16)


def lifted_terms(*args):
    sm = pl.BlockSpec(memory_space=pltpu.SMEM)
    vm = pl.BlockSpec(memory_space=pltpu.VMEM)
    return pl.pallas_call(
        terms_kernel,
        out_shape=(
            jax.ShapeDtypeStruct((8, 8, 32, 128), BF16),
            jax.ShapeDtypeStruct((8, 256), F32),
            jax.ShapeDtypeStruct((4, 128, 128), BF16),
        ),
        in_specs=[sm] * 4 + [vm] * 7,
        out_specs=(vm, vm, vm),
        scratch_shapes=[
            pltpu.VMEM((16, 4096, 128), BF16),
            pltpu.VMEM((4096, 64), BF16),
            pltpu.VMEM((64, 128, 128), F32),
            pltpu.VMEM((64, 128), F32),
            pltpu.VMEM((4, 64, 128), F32),
            pltpu.VMEM((16, 8, 128), F32),
            pltpu.VMEM((32 * 64, 128), F32),
            pltpu.SMEM((33,), jnp.int32),
            pltpu.SMEM((33,), jnp.int32),
            pltpu.SMEM((16,), jnp.int32),
        ],
        compiler_params=pltpu.CompilerParams(vmem_limit_bytes=VMEM_BYTES),
        name="slot_terms",
    )(*args)


def modes_value(tag_col, tag_row, terms, z_hi, z_lo, xy):
    lane = lax.broadcasted_iota(jnp.int32, (256, 256), 1)
    row = lax.broadcasted_iota(jnp.int32, (256, 256), 0)
    same = jnp.logical_and(tag_col == tag_row, tag_row >= 0)
    before = jnp.logical_and(same, lane < row)
    early = jnp.max(jnp.where(before, 1.0, 0.0), axis=1, keepdims=True)
    leader = jnp.where(tag_col[:, :1] >= 0, 1.0 - early, 0.0)
    sums = jnp.dot(jnp.where(same, 1.0, 0.0).astype(BF16), terms, preferred_element_type=F32)
    inner = math.sqrt(2.0 / math.pi) * (sums + 0.044715 * (sums * sums * sums))
    acts = (0.5 * leader) * (sums * (1.0 + jnp.tanh(inner)))
    z_lane = lax.broadcasted_iota(jnp.int32, (128, 256), 1) // 32
    zero = jnp.zeros((128, 256), BF16)
    zm = jnp.zeros((256, 256), F32)
    for e in range(8):
        pick = z_lane == e
        zm = zm + dot3(
            split(acts[:, e * 128 : (e + 1) * 128]),
            (jnp.where(pick, z_hi, zero), jnp.where(pick, z_lo, zero)),
        )
    imag_lane = (lane // 16) % 2 == 1
    swapped = jnp.where(imag_lane, pltpu.roll(zm, 16, 1), -pltpu.roll(zm, 240, 1))
    tag = jnp.maximum(tag_row, 0)
    pos = row % 128
    hot_x = jnp.where(pos == tag // 128, 1.0, 0.0).astype(BF16)
    hot_y = jnp.where(pos == tag % 128, 1.0, 0.0).astype(BF16)
    by_x = jnp.dot(xy[:512], hot_x, preferred_element_type=F32)
    by_y = jnp.dot(xy[512:], hot_y, preferred_element_type=F32)
    cos_x, sin_x, cos_y, sin_y = by_x[:256], by_x[256:], by_y[:256], by_y[256:]
    cos_part = cos_x * cos_y - sin_x * sin_y
    sin_part = -(sin_x * cos_y + cos_x * sin_y)
    out = dot3(split(cos_part), split(zm)) + dot3(split(sin_part), split(swapped))
    return out * (1.0 / math.sqrt(32768.0))


def swap_rows_runs(x):
    rows, lanes = x.shape
    row = lax.broadcasted_iota(jnp.int32, x.shape, 0) % 8
    run = (lax.broadcasted_iota(jnp.int32, x.shape, 1) % 128) // 16
    for step in (1, 2, 4):
        row_bit = (row // step) % 2
        run_bit = (run // step) % 2
        down = pltpu.roll(pltpu.roll(x, lanes - 16 * step, 1), step, 0)
        up = pltpu.roll(pltpu.roll(x, 16 * step, 1), rows - step, 0)
        x = jnp.where(row_bit == run_bit, x, jnp.where(row_bit == 1, down, up))
    return x


def exchange_kernel(
    terms, tags, cot, z_hi, z_lo, xy, out,
    terms_in, tags_in, cot_in, x_out, x_mid, x_in, pick, g_out, g_in, fold,
    t_send, t_recv, n_send, n_recv, c_send, c_recv, b_send, b_recv, y_send, y_recv, x_send, x_recv, g_send, g_recv,
):
    dp = lax.axis_index("dp")
    slab = lax.axis_index("slab")
    z = dp // 4
    part = dp - z * 4

    def copy_to(src, dst, send, recv, dp_to, slab_to):
        return pltpu.make_async_remote_copy(
            src_ref=src, dst_ref=dst, send_sem=send, recv_sem=recv,
            device_id=(dp_to, slab_to), device_id_type=pl.DeviceIdType.MESH,
        )

    def terms_copy(to):
        return copy_to(terms.at[to], terms_in.at[slab], t_send.at[to], t_recv.at[slab], dp, to)

    def tags_copy(to):
        return copy_to(tags, tags_in.at[slab], n_send.at[to], n_recv.at[slab], dp, to)

    def cot_copy(to):
        return copy_to(cot.at[to], cot_in.at[dp], c_send.at[to], c_recv.at[part], z * 4 + to, slab)

    def block_copy(k, ahead, step):
        src = lax.rem(z + ahead + 8, 8)
        block = cot_in.at[pl.ds(src * 4, 4)]
        to = lax.rem(z + step + 8, 8)
        return copy_to(block, block, b_send.at[k], b_recv.at[src], to * 4 + part, slab)

    block_sends = ((0, 0, 1), (1, 0, -1), (2, -1, 1), (3, 1, -1), (4, -2, 1), (5, 2, -1), (6, -3, 1))

    def wait_block(ahead):
        block_copy(0, ahead, 1).wait_recv()

    def slab_rows(at):
        return x_out.at[:, pl.ds(pl.multiple_of(at * 32, 32), 32)]

    def part_rows(at):
        return x_mid.at[at // 4, :, pl.ds(pl.multiple_of(lax.rem(at, 4) * 8, 8), 8)]

    def y_copy(to):
        return copy_to(slab_rows(to), x_mid.at[slab], y_send.at[to], y_recv.at[slab], dp, to)

    def x_copy(to):
        return copy_to(part_rows(to), x_in.at[dp], x_send.at[to], x_recv.at[dp], to, slab)

    def g_copy(to):
        return copy_to(g_out.at[to], g_in.at[part], g_send.at[to], g_recv.at[part], z * 4 + to, slab)

    own_terms = pltpu.make_async_copy(terms.at[slab], terms_in.at[slab], t_recv.at[slab])
    own_tags = pltpu.make_async_copy(tags, tags_in.at[slab], n_recv.at[slab])
    own_cot = pltpu.make_async_copy(cot.at[part], cot_in.at[dp], c_recv.at[part])
    own_y = pltpu.make_async_copy(slab_rows(slab), x_mid.at[slab], y_recv.at[slab])
    own_x = pltpu.make_async_copy(part_rows(dp), x_in.at[dp], x_recv.at[dp])

    def others(count, me, act):
        def step(i, carry):
            act(lax.rem(me + i, count))
            return carry

        lax.fori_loop(1, count, step, 0)

    barrier = pltpu.get_barrier_semaphore()

    def greet(dp_to, slab_to):
        pl.semaphore_signal(
            barrier, inc=1, device_id=(dp_to, slab_to), device_id_type=pl.DeviceIdType.MESH
        )

    others(8, slab, lambda to: greet(dp, to))
    others(32, dp, lambda to: greet(to, slab))
    pl.semaphore_wait(barrier, 7 + 31)

    own_terms.start()
    own_tags.start()
    own_cot.start()

    def start_slab(to):
        terms_copy(to).start()
        tags_copy(to).start()

    others(4, part, lambda to: cot_copy(to).start())
    others(8, slab, start_slab)
    own_cot.wait()

    def wait_cot(frm):
        copy_to(cot.at[frm], cot_in.at[z * 4 + frm], c_send.at[frm], c_recv.at[frm], z * 4 + frm, slab).wait_recv()

    others(4, part, wait_cot)

    def pass_block(k):
        if k > 1:
            wait_block(block_sends[k][1])
        block_copy(*block_sends[k]).start()

    pass_block(0)
    pass_block(1)

    own_terms.wait()
    own_tags.wait()

    def wait_slab(frm):
        copy_to(terms.at[frm], terms_in.at[frm], t_send.at[frm], t_recv.at[frm], dp, frm).wait_recv()
        copy_to(tags, tags_in.at[frm], n_send.at[frm], n_recv.at[frm], dp, frm).wait_recv()

    others(8, slab, wait_slab)
    pass_block(2)
    pass_block(3)
    t = jnp.concatenate(
        [jnp.concatenate([terms_in[r, e] for r in range(8)], axis=0) for e in range(8)], axis=1
    )
    tag_sum = tags_in[0]
    for r in range(1, 8):
        tag_sum = tag_sum + tags_in[r]
    row = jnp.broadcast_to(tag_sum[0:1, :], (256, 256))
    x = modes_value(row.T.astype(jnp.int32), row.astype(jnp.int32), t, z_hi[...], z_lo[...], xy[...])
    x = swap_rows_runs(x)
    x_out[0] = x[:, :128]
    x_out[1] = x[:, 128:]

    own_y.start()
    others(8, slab, lambda to: y_copy(to).start())
    pass_block(4)
    pass_block(5)

    def pass_on(frm):
        for a in range(4):
            to = frm * 4 + a

            @pl.when(to == dp)
            def _():
                own_x.start()

            @pl.when(to != dp)
            def _():
                x_copy(to).start()

    own_y.wait()
    pass_on(slab)

    def relay(frm):
        copy_to(slab_rows(0), x_mid.at[frm], y_send.at[frm], y_recv.at[frm], dp, frm).wait_recv()
        pass_on(frm)

    others(8, slab, relay)
    pass_block(6)
    for ahead in (3, 4):
        wait_block(ahead)

    def wait_x(frm):
        copy_to(part_rows(0), x_in.at[frm], x_send.at[frm], x_recv.at[frm], frm, slab).wait_recv()

    own_x.wait()
    others(32, dp, wait_x)

    def channels(to):
        both = x_in[:, to // 2]
        pick[...] = jnp.where(lax.rem(to, 2) == 1, pltpu.roll(both, 4, 1), both)
        for o in range(4):
            low = pl.ds(o * 16, 16)
            high = pl.ds(64 + o * 16, 16)

            def sample(s, acc):
                g_low = cot_in[s, low, :].astype(F32)
                g_high = cot_in[s, high, :].astype(F32)
                new = []
                for q in range(4):
                    xq = pick[s, q : q + 1, :]
                    new.append(acc[2 * q] + xq * g_low)
                    new.append(acc[2 * q + 1] + xq * g_high)
                return tuple(new)

            acc = lax.fori_loop(0, 32, sample, tuple(jnp.zeros((16, 128), F32) for _ in range(8)), unroll=4)
            for i in range(2):
                re_low, re_high, im_low, im_high = acc[4 * i : 4 * i + 4]
                fold[i, low, :] = re_low + im_high
                fold[i, high, :] = re_high - im_low
        for i in range(2):
            g_out[to, i] = fold[i].T.astype(BF16)

    def one(k, carry):
        other = (1 - part // 2) * 2 + k
        here = (part // 2) * 2 + lax.rem(part + k + 1, 2)
        to = jnp.where(k < 2, other, here)
        channels(to)

        @pl.when(k < 3)
        def _():
            g_copy(to).start()

        return carry

    lax.fori_loop(0, 4, one, 0)
    out[0, part] = g_out[part, 0]
    out[1, part] = g_out[part, 1]

    def take(frm):
        copy_to(g_out.at[frm], g_in.at[frm], g_send.at[frm], g_recv.at[frm], z * 4 + frm, slab).wait_recv()
        out[0, frm] = g_in[frm, 0]
        out[1, frm] = g_in[frm, 1]

    others(4, part, take)

    def sent_slab(to):
        terms_copy(to).wait_send()
        tags_copy(to).wait_send()

    others(8, slab, sent_slab)
    others(4, part, lambda to: cot_copy(to).wait_send())
    for k in range(7):
        block_copy(*block_sends[k]).wait_send()

    others(8, slab, lambda to: y_copy(to).wait_send())
    others(32, dp, lambda to: x_copy(to).wait_send())
    others(4, part, lambda to: g_copy(to).wait_send())


def exchange(terms, tags, cot):
    z_hi, z_lo, xy = (jnp.asarray(t) for t in tables())
    vm = pl.BlockSpec(memory_space=pltpu.VMEM)
    dma = pltpu.SemaphoreType.DMA
    return pl.pallas_call(
        exchange_kernel,
        out_shape=jax.ShapeDtypeStruct((2, 4, 128, 128), BF16),
        in_specs=[vm] * 6,
        out_specs=vm,
        scratch_shapes=[
            pltpu.VMEM((8, 8, 32, 128), BF16),
            pltpu.VMEM((8, 8, 256), F32),
            pltpu.VMEM((32, 128, 128), BF16),
            pltpu.VMEM((2, 256, 128), F32),
            pltpu.VMEM((8, 2, 32, 128), F32),
            pltpu.VMEM((32, 2, 8, 128), F32),
            pltpu.VMEM((32, 8, 128), F32),
            pltpu.VMEM((4, 2, 128, 128), BF16),
            pltpu.VMEM((4, 2, 128, 128), BF16),
            pltpu.VMEM((2, 128, 128), F32),
            dma((8,)), dma((8,)), dma((8,)), dma((8,)), dma((4,)), dma((4,)), dma((8,)), dma((8,)),
            dma((8,)), dma((8,)), dma((32,)), dma((32,)), dma((4,)), dma((4,)),
        ],
        compiler_params=pltpu.CompilerParams(
            vmem_limit_bytes=VMEM_BYTES, collective_id=0, has_side_effects=True
        ),
        name="exchange",
    )(terms, tags, cot, z_hi, z_lo, xy)


def per_device(
    point_feats, point_coords, slot_block, slot_cell, slot_count, cotangent,
    offset_map, offset_bias, kernel_mix, lift_weight,
):
    terms, tags, cot = lifted_terms(
        slot_block[0, 0].T, slot_cell[0, 0].T, slot_count[0], offset_map.T,
        point_feats[0], point_coords[0].transpose(1, 0, 2), kernel_mix, offset_map.T, offset_bias[None, :], lift_weight,
        cotangent.reshape(512, 128),
    )
    grad = exchange(terms, tags, cot)
    return grad.astype(F32).reshape(2, 2, 16, 16, 128)


def solution(mesh):
    placed = (
        P("dp", "slab", None, None), P("dp", "slab", None, None), P("dp", "slab", None, None),
        P("dp", "slab", None, None), P("dp", "slab", None), P("dp", "slab", None, None, None),
        P(), P(), P(), P(),
    )
    return jax.shard_map(
        per_device,
        mesh=mesh,
        in_specs=placed,
        out_specs=P("dp", "slab", None, None, None),
        check_vma=False,
    )
```

```python
import math

import jax
import jax.numpy as jnp
import numpy as np
from jax import lax
from jax.experimental import pallas as pl
from jax.experimental.pallas import tpu as pltpu
from jax.sharding import PartitionSpec as P

F32 = jnp.float32
BF16 = jnp.bfloat16
NT = (((1,), (1,)), ((), ()))
VMEM_BYTES = 60 * 2**20


def split(x):
    hi = x.astype(BF16)
    return hi, (x - hi.astype(F32)).astype(BF16)


def dot3(a, b):
    ah, al = a
    bh, bl = b
    out = jnp.dot(ah, bh, preferred_element_type=F32)
    out = out + jnp.dot(al, bh, preferred_element_type=F32)
    return out + jnp.dot(ah, bl, preferred_element_type=F32)


def np_split(x):
    hi = np.asarray(x, np.float32).astype(BF16)
    lo = (np.asarray(x, np.float64) - hi.astype(np.float64)).astype(BF16)
    return hi, lo


def tables():
    z = np.arange(128)
    k = np.arange(16)
    turn = np.mod(z[:, None] * k[None, :], 128) * (2.0 * np.pi / 128)
    z_table = np.tile(np.concatenate([np.cos(turn), -np.sin(turn)], axis=1), (1, 8))
    z_hi, z_lo = np_split(z_table)
    signed = np.where(k < 8, k, k - 16)
    angle = np.mod(signed[:, None] * z[None, :], 128) * (2.0 * np.pi / 128)
    by_x = np.repeat(angle, 16, axis=0)
    by_y = np.tile(angle, (16, 1))
    xy = []
    for part in (np.cos(by_x), np.sin(by_x), np.cos(by_y), np.sin(by_y)):
        xy.append(np.concatenate(np_split(part), axis=1))
    return z_hi, z_lo, np.concatenate(xy, axis=0)


def terms_kernel(
    blk, cel, cnt, om, feats, coords, kmix, coef_ref, bias_ref, lift_ref, cot,
    out, tags, cot_out, mixed, mix, tab, base, coef, points, sums, lifted, live, todo, seen,
):
    for b in range(16):
        seen[b] = 0

    def scan(n, carry):
        n_live, n_todo = carry
        slab = n // 4
        j = n - slab * 4
        is_live = j < cnt[0, slab]
        b = blk[j, slab]
        fresh = jnp.logical_and(is_live, seen[b] == 0)
        live[n_live] = n
        todo[n_todo] = b
        seen[b] = jnp.where(is_live, 1, seen[b])
        return n_live + is_live.astype(jnp.int32), n_todo + fresh.astype(jnp.int32)

    n_live, n_todo = lax.fori_loop(0, 32, scan, (jnp.int32(0), jnp.int32(0)))
    place = lax.broadcasted_iota(jnp.int32, (8, 256), 1) - 32 * lax.axis_index("slab")
    tag = jnp.zeros((8, 256), F32)
    for n in range(32):
        value = jnp.where(n % 4 < cnt[0, n // 4], (n // 4) * 2048 + cel[n % 4, n // 4], -1).astype(F32)
        tag = jnp.where(place == n, value, tag)
    tags[...] = tag
    for a in range(4):
        cot_out[a] = cot[a * 128 : (a + 1) * 128, :].T.astype(BF16)
    for h in range(32):
        both = jnp.concatenate([kmix[2 * h], kmix[2 * h + 1]], axis=1).astype(F32)
        mix[h * 128 : (h + 1) * 128, :] = both.T.astype(BF16)
    lifted[...] = jnp.zeros_like(lifted)
    pos_z = (lax.broadcasted_iota(jnp.int32, (128, 128), 0).astype(F32) + 0.5) * (1.0 / 128)

    def fill(h, carry):
        tab[h] = pos_z * om[2, h]
        return carry

    lax.fori_loop(0, 64, fill, 0)

    def mix_pair(i, carry):
        b0 = todo[2 * i]
        b1 = todo[jnp.minimum(2 * i + 1, n_todo - 1)]
        pair = jnp.concatenate([feats[b0], feats[b1]], axis=1)

        def rows(r, carry):
            start = pl.multiple_of(r * 2048, 2048)
            m = jnp.dot(mix[pl.ds(start, 2048), :], pair, preferred_element_type=F32).astype(BF16)
            mixed[b0, pl.ds(start, 2048), :] = m[:, :128]
            mixed[b1, pl.ds(start, 2048), :] = m[:, 128:]
            return carry

        return lax.fori_loop(0, 2, rows, carry)

    lax.fori_loop(0, (n_todo + 1) // 2, mix_pair, 0)
    for c in range(3):
        coef[c] = jnp.broadcast_to(coef_ref[c : c + 1, :], (128, 64)).T
    coef[3] = jnp.broadcast_to(bias_ref[...], (128, 64)).T
    for c in range(3):
        by_block = coords[c].astype(F32)
        for b in range(16):
            points[b, c : c + 1, :] = by_block[b : b + 1, :]
    lift_v = lift_ref[...].astype(F32).T.astype(BF16)

    def slot(i, carry):
        n = live[i]
        slab = n // 4
        b = blk[n - slab * 4, slab]
        cell = cel[n - slab * 4, slab]
        x = slab * 16 + cell // 128
        y = lax.rem(cell, 128)
        pos_x = (x.astype(F32) + 0.5) * (1.0 / 128)
        pos_y = (y.astype(F32) + 0.5) * (1.0 / 128)
        coef_x, coef_y, coef_z = coef[0], coef[1], coef[2]
        point = coef_x * points[b, 0:1] + coef_y * points[b, 1:2] + coef_z * points[b, 2:3]
        base[...] = (coef_x * pos_x + coef_y * pos_y) + coef[3] - point
        ws, ms = [], []
        for h in range(64):
            w = (tab[h] + base[pl.ds(h, 1), :]).astype(BF16)
            ws.append(jnp.maximum(w, jnp.zeros_like(w)))
            ms.append(mixed[b, h * 64 : (h + 1) * 64, :])
        total = lax.dot_general(
            jnp.concatenate(ws, axis=1), jnp.concatenate(ms, axis=1), NT, preferred_element_type=F32
        )
        sums[i] = total
        return carry

    lax.fori_loop(0, n_live, slot, 0)

    def lift_four(g, carry):
        for u in range(4):
            i = jnp.minimum(4 * g + u, n_live - 1)
            hi, lo = split(sums[i].T * (1.0 / 128))
            pre = jnp.dot(lift_v, hi, preferred_element_type=F32) + jnp.dot(lift_v, lo, preferred_element_type=F32)
            lifted[pl.ds(pl.multiple_of(live[i] * 64, 64), 64), :] = pre
        return carry

    lax.fori_loop(0, (n_live + 3) // 4, lift_four, 0)
    for e in range(64):
        out[e // 8, e % 8] = lifted[pl.ds(e, 32, stride=64), :].astype(BF16)


def lifted_terms(*args):
    sm = pl.BlockSpec(memory_space=pltpu.SMEM)
    vm = pl.BlockSpec(memory_space=pltpu.VMEM)
    return pl.pallas_call(
        terms_kernel,
        out_shape=(
            jax.ShapeDtypeStruct((8, 8, 32, 128), BF16),
            jax.ShapeDtypeStruct((8, 256), F32),
            jax.ShapeDtypeStruct((4, 128, 128), BF16),
        ),
        in_specs=[sm] * 4 + [vm] * 7,
        out_specs=(vm, vm, vm),
        scratch_shapes=[
            pltpu.VMEM((16, 4096, 128), BF16),
            pltpu.VMEM((4096, 64), BF16),
            pltpu.VMEM((64, 128, 128), F32),
            pltpu.VMEM((64, 128), F32),
            pltpu.VMEM((4, 64, 128), F32),
            pltpu.VMEM((16, 8, 128), F32),
            pltpu.VMEM((32, 128, 64), F32),
            pltpu.VMEM((32 * 64, 128), F32),
            pltpu.SMEM((33,), jnp.int32),
            pltpu.SMEM((33,), jnp.int32),
            pltpu.SMEM((16,), jnp.int32),
        ],
        compiler_params=pltpu.CompilerParams(vmem_limit_bytes=VMEM_BYTES),
        name="slot_terms",
    )(*args)


def modes_value(tag_col, tag_row, terms, z_hi, z_lo, xy):
    lane = lax.broadcasted_iota(jnp.int32, (256, 256), 1)
    row = lax.broadcasted_iota(jnp.int32, (256, 256), 0)
    same = jnp.logical_and(tag_col == tag_row, tag_row >= 0)
    before = jnp.logical_and(same, lane < row)
    early = jnp.max(jnp.where(before, 1.0, 0.0), axis=1, keepdims=True)
    leader = jnp.where(tag_col[:, :1] >= 0, 1.0 - early, 0.0)
    sums = jnp.dot(jnp.where(same, 1.0, 0.0).astype(BF16), terms, preferred_element_type=F32)
    inner = math.sqrt(2.0 / math.pi) * (sums + 0.044715 * (sums * sums * sums))
    acts = (0.5 * leader) * (sums * (1.0 + jnp.tanh(inner)))
    z_lane = lax.broadcasted_iota(jnp.int32, (128, 256), 1) // 32
    zero = jnp.zeros((128, 256), BF16)
    zm = jnp.zeros((256, 256), F32)
    for e in range(8):
        pick = z_lane == e
        zm = zm + dot3(
            split(acts[:, e * 128 : (e + 1) * 128]),
            (jnp.where(pick, z_hi, zero), jnp.where(pick, z_lo, zero)),
        )
    imag_lane = (lane // 16) % 2 == 1
    swapped = jnp.where(imag_lane, pltpu.roll(zm, 16, 1), -pltpu.roll(zm, 240, 1))
    tag = jnp.maximum(tag_row, 0)
    pos = row % 128
    hot_x = jnp.where(pos == tag // 128, 1.0, 0.0).astype(BF16)
    hot_y = jnp.where(pos == tag % 128, 1.0, 0.0).astype(BF16)
    by_x = jnp.dot(xy[:512], hot_x, preferred_element_type=F32)
    by_y = jnp.dot(xy[512:], hot_y, preferred_element_type=F32)
    cos_x, sin_x, cos_y, sin_y = by_x[:256], by_x[256:], by_y[:256], by_y[256:]
    cos_part = cos_x * cos_y - sin_x * sin_y
    sin_part = -(sin_x * cos_y + cos_x * sin_y)
    out = dot3(split(cos_part), split(zm)) + dot3(split(sin_part), split(swapped))
    return out * (1.0 / math.sqrt(32768.0))


def swap_rows_runs(x):
    rows, lanes = x.shape
    row = lax.broadcasted_iota(jnp.int32, x.shape, 0) % 8
    run = (lax.broadcasted_iota(jnp.int32, x.shape, 1) % 128) // 16
    for step in (1, 2, 4):
        row_bit = (row // step) % 2
        run_bit = (run // step) % 2
        down = pltpu.roll(pltpu.roll(x, lanes - 16 * step, 1), step, 0)
        up = pltpu.roll(pltpu.roll(x, 16 * step, 1), rows - step, 0)
        x = jnp.where(row_bit == run_bit, x, jnp.where(row_bit == 1, down, up))
    return x


def exchange_kernel(
    terms, tags, cot, z_hi, z_lo, xy, out,
    terms_in, tags_in, cot_in, x_out, x_mid, x_in, pick, g_out, g_in, fold,
    t_send, t_recv, n_send, n_recv, c_send, c_recv, b_send, b_recv, y_send, y_recv, x_send, x_recv, g_send, g_recv,
):
    dp = lax.axis_index("dp")
    slab = lax.axis_index("slab")
    z = dp // 4
    part = dp - z * 4

    def copy_to(src, dst, send, recv, dp_to, slab_to):
        return pltpu.make_async_remote_copy(
            src_ref=src, dst_ref=dst, send_sem=send, recv_sem=recv,
            device_id=(dp_to, slab_to), device_id_type=pl.DeviceIdType.MESH,
        )

    def terms_copy(to):
        return copy_to(terms.at[to], terms_in.at[slab], t_send.at[to], t_recv.at[slab], dp, to)

    def tags_copy(to):
        return copy_to(tags, tags_in.at[slab], n_send.at[to], n_recv.at[slab], dp, to)

    def cot_copy(to):
        return copy_to(cot.at[to], cot_in.at[dp], c_send.at[to], c_recv.at[part], z * 4 + to, slab)

    def block_copy(k, ahead, step):
        src = lax.rem(z + ahead + 8, 8)
        block = cot_in.at[pl.ds(src * 4, 4)]
        to = lax.rem(z + step + 8, 8)
        return copy_to(block, block, b_send.at[k], b_recv.at[src], to * 4 + part, slab)

    block_sends = ((0, 0, 1), (1, 0, -1), (2, -1, 1), (3, 1, -1), (4, -2, 1), (5, 2, -1), (6, -3, 1))

    def wait_block(ahead):
        block_copy(0, ahead, 1).wait_recv()

    def slab_rows(at):
        return x_out.at[:, pl.ds(pl.multiple_of(at * 32, 32), 32)]

    def part_rows(at):
        return x_mid.at[at // 4, :, pl.ds(pl.multiple_of(lax.rem(at, 4) * 8, 8), 8)]

    def y_copy(to):
        return copy_to(slab_rows(to), x_mid.at[slab], y_send.at[to], y_recv.at[slab], dp, to)

    def x_copy(to):
        return copy_to(part_rows(to), x_in.at[dp], x_send.at[to], x_recv.at[dp], to, slab)

    def g_copy(to):
        return copy_to(g_out.at[to], g_in.at[part], g_send.at[to], g_recv.at[part], z * 4 + to, slab)

    own_terms = pltpu.make_async_copy(terms.at[slab], terms_in.at[slab], t_recv.at[slab])
    own_tags = pltpu.make_async_copy(tags, tags_in.at[slab], n_recv.at[slab])
    own_cot = pltpu.make_async_copy(cot.at[part], cot_in.at[dp], c_recv.at[part])
    own_y = pltpu.make_async_copy(slab_rows(slab), x_mid.at[slab], y_recv.at[slab])
    own_x = pltpu.make_async_copy(part_rows(dp), x_in.at[dp], x_recv.at[dp])

    def others(count, me, act):
        def step(i, carry):
            act(lax.rem(me + i, count))
            return carry

        lax.fori_loop(1, count, step, 0)

    barrier = pltpu.get_barrier_semaphore()

    def greet(dp_to, slab_to):
        pl.semaphore_signal(
            barrier, inc=1, device_id=(dp_to, slab_to), device_id_type=pl.DeviceIdType.MESH
        )

    others(8, slab, lambda to: greet(dp, to))
    others(32, dp, lambda to: greet(to, slab))
    pl.semaphore_wait(barrier, 7 + 31)

    own_terms.start()
    own_tags.start()
    own_cot.start()

    def start_slab(to):
        terms_copy(to).start()
        tags_copy(to).start()

    others(4, part, lambda to: cot_copy(to).start())
    others(8, slab, start_slab)
    own_cot.wait()

    def wait_cot(frm):
        copy_to(cot.at[frm], cot_in.at[z * 4 + frm], c_send.at[frm], c_recv.at[frm], z * 4 + frm, slab).wait_recv()

    others(4, part, wait_cot)

    def pass_block(k):
        if k > 1:
            wait_block(block_sends[k][1])
        block_copy(*block_sends[k]).start()

    pass_block(0)
    pass_block(1)

    own_terms.wait()
    own_tags.wait()

    def wait_slab(frm):
        copy_to(terms.at[frm], terms_in.at[frm], t_send.at[frm], t_recv.at[frm], dp, frm).wait_recv()
        copy_to(tags, tags_in.at[frm], n_send.at[frm], n_recv.at[frm], dp, frm).wait_recv()

    others(8, slab, wait_slab)
    pass_block(2)
    pass_block(3)
    t = jnp.concatenate(
        [jnp.concatenate([terms_in[r, e] for r in range(8)], axis=0) for e in range(8)], axis=1
    )
    tag_sum = tags_in[0]
    for r in range(1, 8):
        tag_sum = tag_sum + tags_in[r]
    row = jnp.broadcast_to(tag_sum[0:1, :], (256, 256))
    x = modes_value(row.T.astype(jnp.int32), row.astype(jnp.int32), t, z_hi[...], z_lo[...], xy[...])
    x = swap_rows_runs(x)
    x_out[0] = x[:, :128]
    x_out[1] = x[:, 128:]

    own_y.start()
    others(8, slab, lambda to: y_copy(to).start())
    pass_block(4)
    pass_block(5)

    def pass_on(frm):
        for a in range(4):
            to = frm * 4 + a

            @pl.when(to == dp)
            def _():
                own_x.start()

            @pl.when(to != dp)
            def _():
                x_copy(to).start()

    own_y.wait()
    pass_on(slab)

    def relay(frm):
        copy_to(slab_rows(0), x_mid.at[frm], y_send.at[frm], y_recv.at[frm], dp, frm).wait_recv()
        pass_on(frm)

    others(8, slab, relay)
    pass_block(6)
    for ahead in (3, 4):
        wait_block(ahead)

    def wait_x(frm):
        copy_to(part_rows(0), x_in.at[frm], x_send.at[frm], x_recv.at[frm], frm, slab).wait_recv()

    own_x.wait()
    others(32, dp, wait_x)

    def channels(to):
        both = x_in[:, to // 2]
        pick[...] = jnp.where(lax.rem(to, 2) == 1, pltpu.roll(both, 4, 1), both)
        for o in range(4):
            low = pl.ds(o * 16, 16)
            high = pl.ds(64 + o * 16, 16)

            def sample(s, acc):
                g_low = cot_in[s, low, :].astype(F32)
                g_high = cot_in[s, high, :].astype(F32)
                new = []
                for q in range(4):
                    xq = pick[s, q : q + 1, :]
                    new.append(acc[2 * q] + xq * g_low)
                    new.append(acc[2 * q + 1] + xq * g_high)
                return tuple(new)

            acc = lax.fori_loop(0, 32, sample, tuple(jnp.zeros((16, 128), F32) for _ in range(8)), unroll=4)
            for i in range(2):
                re_low, re_high, im_low, im_high = acc[4 * i : 4 * i + 4]
                fold[i, low, :] = re_low + im_high
                fold[i, high, :] = re_high - im_low
        for i in range(2):
            g_out[to, i] = fold[i].T.astype(BF16)

    def one(k, carry):
        other = (1 - part // 2) * 2 + k
        here = (part // 2) * 2 + lax.rem(part + k + 1, 2)
        to = jnp.where(k < 2, other, here)
        channels(to)

        @pl.when(k < 3)
        def _():
            g_copy(to).start()

        return carry

    lax.fori_loop(0, 4, one, 0)
    out[0, part] = g_out[part, 0]
    out[1, part] = g_out[part, 1]

    def take(frm):
        copy_to(g_out.at[frm], g_in.at[frm], g_send.at[frm], g_recv.at[frm], z * 4 + frm, slab).wait_recv()
        out[0, frm] = g_in[frm, 0]
        out[1, frm] = g_in[frm, 1]

    others(4, part, take)

    def sent_slab(to):
        terms_copy(to).wait_send()
        tags_copy(to).wait_send()

    others(8, slab, sent_slab)
    others(4, part, lambda to: cot_copy(to).wait_send())
    for k in range(7):
        block_copy(*block_sends[k]).wait_send()

    others(8, slab, lambda to: y_copy(to).wait_send())
    others(32, dp, lambda to: x_copy(to).wait_send())
    others(4, part, lambda to: g_copy(to).wait_send())


def exchange(terms, tags, cot):
    z_hi, z_lo, xy = (jnp.asarray(t) for t in tables())
    vm = pl.BlockSpec(memory_space=pltpu.VMEM)
    dma = pltpu.SemaphoreType.DMA
    return pl.pallas_call(
        exchange_kernel,
        out_shape=jax.ShapeDtypeStruct((2, 4, 128, 128), BF16),
        in_specs=[vm] * 6,
        out_specs=vm,
        scratch_shapes=[
            pltpu.VMEM((8, 8, 32, 128), BF16),
            pltpu.VMEM((8, 8, 256), F32),
            pltpu.VMEM((32, 128, 128), BF16),
            pltpu.VMEM((2, 256, 128), F32),
            pltpu.VMEM((8, 2, 32, 128), F32),
            pltpu.VMEM((32, 2, 8, 128), F32),
            pltpu.VMEM((32, 8, 128), F32),
            pltpu.VMEM((4, 2, 128, 128), BF16),
            pltpu.VMEM((4, 2, 128, 128), BF16),
            pltpu.VMEM((2, 128, 128), F32),
            dma((8,)), dma((8,)), dma((8,)), dma((8,)), dma((4,)), dma((4,)), dma((8,)), dma((8,)),
            dma((8,)), dma((8,)), dma((32,)), dma((32,)), dma((4,)), dma((4,)),
        ],
        compiler_params=pltpu.CompilerParams(
            vmem_limit_bytes=VMEM_BYTES, collective_id=0, has_side_effects=True
        ),
        name="exchange",
    )(terms, tags, cot, z_hi, z_lo, xy)


def per_device(
    point_feats, point_coords, slot_block, slot_cell, slot_count, cotangent,
    offset_map, offset_bias, kernel_mix, lift_weight,
):
    terms, tags, cot = lifted_terms(
        slot_block[0, 0].T, slot_cell[0, 0].T, slot_count[0], offset_map.T,
        point_feats[0], point_coords[0].transpose(1, 0, 2), kernel_mix, offset_map.T, offset_bias[None, :], lift_weight,
        cotangent.reshape(512, 128),
    )
    grad = exchange(terms, tags, cot)
    return grad.astype(F32).reshape(2, 2, 16, 16, 128)


def solution(mesh):
    placed = (
        P("dp", "slab", None, None), P("dp", "slab", None, None), P("dp", "slab", None, None),
        P("dp", "slab", None, None), P("dp", "slab", None), P("dp", "slab", None, None, None),
        P(), P(), P(), P(),
    )
    return jax.shard_map(
        per_device,
        mesh=mesh,
        in_specs=placed,
        out_specs=P("dp", "slab", None, None, None),
        check_vma=False,
    )
```

```python
import math

import jax
import jax.numpy as jnp
import numpy as np
from jax import lax
from jax.experimental import pallas as pl
from jax.experimental.pallas import tpu as pltpu
from jax.sharding import PartitionSpec as P

F32 = jnp.float32
BF16 = jnp.bfloat16
NT = (((1,), (1,)), ((), ()))
VMEM_BYTES = 60 * 2**20


def split(x):
    hi = x.astype(BF16)
    return hi, (x - hi.astype(F32)).astype(BF16)


def dot3(a, b):
    ah, al = a
    bh, bl = b
    out = jnp.dot(ah, bh, preferred_element_type=F32)
    out = out + jnp.dot(al, bh, preferred_element_type=F32)
    return out + jnp.dot(ah, bl, preferred_element_type=F32)


def np_split(x):
    hi = np.asarray(x, np.float32).astype(BF16)
    lo = (np.asarray(x, np.float64) - hi.astype(np.float64)).astype(BF16)
    return hi, lo


def tables():
    z = np.arange(128)
    k = np.arange(16)
    turn = np.mod(z[:, None] * k[None, :], 128) * (2.0 * np.pi / 128)
    z_table = np.tile(np.concatenate([np.cos(turn), -np.sin(turn)], axis=1), (1, 8))
    z_hi, z_lo = np_split(z_table)
    signed = np.where(k < 8, k, k - 16)
    angle = np.mod(signed[:, None] * z[None, :], 128) * (2.0 * np.pi / 128)
    by_x = np.repeat(angle, 16, axis=0)
    by_y = np.tile(angle, (16, 1))
    xy = []
    for part in (np.cos(by_x), np.sin(by_x), np.cos(by_y), np.sin(by_y)):
        xy.append(np.concatenate(np_split(part), axis=1))
    return z_hi, z_lo, np.concatenate(xy, axis=0)


def terms_kernel(
    blk, cel, cnt, om, feats, coords, kmix, coef_ref, bias_ref, lift_ref, cot,
    out, tags, cot_out, mixed, mix, tab, base, coef, points, sums, lifted, live, todo, seen,
):
    for b in range(16):
        seen[b] = 0

    def scan(n, carry):
        n_live, n_todo = carry
        slab = n // 4
        j = n - slab * 4
        is_live = j < cnt[0, slab]
        b = blk[j, slab]
        fresh = jnp.logical_and(is_live, seen[b] == 0)
        live[n_live] = n
        todo[n_todo] = b
        seen[b] = jnp.where(is_live, 1, seen[b])
        return n_live + is_live.astype(jnp.int32), n_todo + fresh.astype(jnp.int32)

    n_live, n_todo = lax.fori_loop(0, 32, scan, (jnp.int32(0), jnp.int32(0)))
    place = lax.broadcasted_iota(jnp.int32, (8, 256), 1) - 32 * lax.axis_index("slab")
    tag = jnp.zeros((8, 256), F32)
    for n in range(32):
        value = jnp.where(n % 4 < cnt[0, n // 4], (n // 4) * 2048 + cel[n % 4, n // 4], -1).astype(F32)
        tag = jnp.where(place == n, value, tag)
    tags[...] = tag
    for a in range(4):
        cot_out[a] = cot[a * 128 : (a + 1) * 128, :].T.astype(BF16)
    for h in range(32):
        both = jnp.concatenate([kmix[2 * h], kmix[2 * h + 1]], axis=1).astype(F32)
        mix[h * 128 : (h + 1) * 128, :] = both.T.astype(BF16)
    lifted[...] = jnp.zeros_like(lifted)
    pos_z = (lax.broadcasted_iota(jnp.int32, (128, 128), 0).astype(F32) + 0.5) * (1.0 / 128)

    def fill(g, carry):
        for u in range(8):
            tab[8 * g + u] = pos_z * om[2, 8 * g + u]
        return carry

    lax.fori_loop(0, 8, fill, 0)

    def mix_pair(i, carry):
        b0 = todo[2 * i]
        b1 = todo[jnp.minimum(2 * i + 1, n_todo - 1)]
        pair = jnp.concatenate([feats[b0], feats[b1]], axis=1)

        def rows(r, carry):
            start = pl.multiple_of(r * 4096, 4096)
            m = jnp.dot(mix[pl.ds(start, 4096), :], pair, preferred_element_type=F32).astype(BF16)
            mixed[b0, pl.ds(start, 4096), :] = m[:, :128]
            mixed[b1, pl.ds(start, 4096), :] = m[:, 128:]
            return carry

        return lax.fori_loop(0, 1, rows, carry)

    lax.fori_loop(0, (n_todo + 1) // 2, mix_pair, 0)
    for c in range(3):
        coef[c] = jnp.broadcast_to(coef_ref[c : c + 1, :], (128, 64)).T
    coef[3] = jnp.broadcast_to(bias_ref[...], (128, 64)).T
    for c in range(3):
        by_block = coords[c].astype(F32)
        for b in range(16):
            points[b, c : c + 1, :] = by_block[b : b + 1, :]
    lift_v = lift_ref[...].astype(F32).T.astype(BF16)

    def slot(i, carry):
        n = live[i]
        slab = n // 4
        b = blk[n - slab * 4, slab]
        cell = cel[n - slab * 4, slab]
        x = slab * 16 + cell // 128
        y = lax.rem(cell, 128)
        pos_x = (x.astype(F32) + 0.5) * (1.0 / 128)
        pos_y = (y.astype(F32) + 0.5) * (1.0 / 128)
        coef_x, coef_y, coef_z = coef[0], coef[1], coef[2]
        point = coef_x * points[b, 0:1] + coef_y * points[b, 1:2] + coef_z * points[b, 2:3]
        base[...] = (coef_x * pos_x + coef_y * pos_y) + coef[3] - point
        ws, ms = [], []
        for h in range(64):
            w = (tab[h] + base[pl.ds(h, 1), :]).astype(BF16)
            ws.append(jnp.maximum(w, jnp.zeros_like(w)))
            ms.append(mixed[b, h * 64 : (h + 1) * 64, :])
        total = lax.dot_general(
            jnp.concatenate(ws, axis=1), jnp.concatenate(ms, axis=1), NT, preferred_element_type=F32
        )
        sums[i] = total
        return carry

    lax.fori_loop(0, n_live, slot, 0)

    def lift_four(g, carry):
        for u in range(4):
            i = jnp.minimum(4 * g + u, n_live - 1)
            hi, lo = split(sums[i].T * (1.0 / 128))
            pre = jnp.dot(lift_v, hi, preferred_element_type=F32) + jnp.dot(lift_v, lo, preferred_element_type=F32)
            lifted[pl.ds(pl.multiple_of(live[i] * 64, 64), 64), :] = pre
        return carry

    lax.fori_loop(0, (n_live + 3) // 4, lift_four, 0)
    for e in range(64):
        out[e // 8, e % 8] = lifted[pl.ds(e, 32, stride=64), :].astype(BF16)


def lifted_terms(*args):
    sm = pl.BlockSpec(memory_space=pltpu.SMEM)
    vm = pl.BlockSpec(memory_space=pltpu.VMEM)
    return pl.pallas_call(
        terms_kernel,
        out_shape=(
            jax.ShapeDtypeStruct((8, 8, 32, 128), BF16),
            jax.ShapeDtypeStruct((8, 256), F32),
            jax.ShapeDtypeStruct((4, 128, 128), BF16),
        ),
        in_specs=[sm] * 4 + [vm] * 7,
        out_specs=(vm, vm, vm),
        scratch_shapes=[
            pltpu.VMEM((16, 4096, 128), BF16),
            pltpu.VMEM((4096, 64), BF16),
            pltpu.VMEM((64, 128, 128), F32),
            pltpu.VMEM((64, 128), F32),
            pltpu.VMEM((4, 64, 128), F32),
            pltpu.VMEM((16, 8, 128), F32),
            pltpu.VMEM((32, 128, 64), F32),
            pltpu.VMEM((32 * 64, 128), F32),
            pltpu.SMEM((33,), jnp.int32),
            pltpu.SMEM((33,), jnp.int32),
            pltpu.SMEM((16,), jnp.int32),
        ],
        compiler_params=pltpu.CompilerParams(vmem_limit_bytes=VMEM_BYTES),
        name="slot_terms",
    )(*args)


def modes_value(tag_col, tag_row, terms, z_hi, z_lo, xy):
    lane = lax.broadcasted_iota(jnp.int32, (256, 256), 1)
    row = lax.broadcasted_iota(jnp.int32, (256, 256), 0)
    same = jnp.logical_and(tag_col == tag_row, tag_row >= 0)
    before = jnp.logical_and(same, lane < row)
    early = jnp.max(jnp.where(before, 1.0, 0.0), axis=1, keepdims=True)
    leader = jnp.where(tag_col[:, :1] >= 0, 1.0 - early, 0.0)
    sums = jnp.dot(jnp.where(same, 1.0, 0.0).astype(BF16), terms, preferred_element_type=F32)
    inner = math.sqrt(2.0 / math.pi) * (sums + 0.044715 * (sums * sums * sums))
    acts = (0.5 * leader) * (sums * (1.0 + jnp.tanh(inner)))
    z_lane = lax.broadcasted_iota(jnp.int32, (128, 256), 1) // 32
    zero = jnp.zeros((128, 256), BF16)
    zm = jnp.zeros((256, 256), F32)
    for e in range(8):
        pick = z_lane == e
        zm = zm + dot3(
            split(acts[:, e * 128 : (e + 1) * 128]),
            (jnp.where(pick, z_hi, zero), jnp.where(pick, z_lo, zero)),
        )
    imag_lane = (lane // 16) % 2 == 1
    swapped = jnp.where(imag_lane, pltpu.roll(zm, 16, 1), -pltpu.roll(zm, 240, 1))
    tag = jnp.maximum(tag_row, 0)
    pos = row % 128
    hot_x = jnp.where(pos == tag // 128, 1.0, 0.0).astype(BF16)
    hot_y = jnp.where(pos == tag % 128, 1.0, 0.0).astype(BF16)
    by_x = jnp.dot(xy[:512], hot_x, preferred_element_type=F32)
    by_y = jnp.dot(xy[512:], hot_y, preferred_element_type=F32)
    cos_x, sin_x, cos_y, sin_y = by_x[:256], by_x[256:], by_y[:256], by_y[256:]
    cos_part = cos_x * cos_y - sin_x * sin_y
    sin_part = -(sin_x * cos_y + cos_x * sin_y)
    out = dot3(split(cos_part), split(zm)) + dot3(split(sin_part), split(swapped))
    return out * (1.0 / math.sqrt(32768.0))


def swap_rows_runs(x):
    rows, lanes = x.shape
    row = lax.broadcasted_iota(jnp.int32, x.shape, 0) % 8
    run = (lax.broadcasted_iota(jnp.int32, x.shape, 1) % 128) // 16
    for step in (1, 2, 4):
        row_bit = (row // step) % 2
        run_bit = (run // step) % 2
        down = pltpu.roll(pltpu.roll(x, lanes - 16 * step, 1), step, 0)
        up = pltpu.roll(pltpu.roll(x, 16 * step, 1), rows - step, 0)
        x = jnp.where(row_bit == run_bit, x, jnp.where(row_bit == 1, down, up))
    return x


def exchange_kernel(
    terms, tags, cot, z_hi, z_lo, xy, out,
    terms_in, tags_in, cot_in, x_out, x_mid, x_in, pick, g_out, g_in, fold,
    t_send, t_recv, n_send, n_recv, c_send, c_recv, b_send, b_recv, y_send, y_recv, x_send, x_recv, g_send, g_recv,
):
    dp = lax.axis_index("dp")
    slab = lax.axis_index("slab")
    z = dp // 4
    part = dp - z * 4

    def copy_to(src, dst, send, recv, dp_to, slab_to):
        return pltpu.make_async_remote_copy(
            src_ref=src, dst_ref=dst, send_sem=send, recv_sem=recv,
            device_id=(dp_to, slab_to), device_id_type=pl.DeviceIdType.MESH,
        )

    def terms_copy(to):
        return copy_to(terms.at[to], terms_in.at[slab], t_send.at[to], t_recv.at[slab], dp, to)

    def tags_copy(to):
        return copy_to(tags, tags_in.at[slab], n_send.at[to], n_recv.at[slab], dp, to)

    def cot_copy(to):
        return copy_to(cot.at[to], cot_in.at[dp], c_send.at[to], c_recv.at[part], z * 4 + to, slab)

    def block_copy(k, ahead, step):
        src = lax.rem(z + ahead + 8, 8)
        block = cot_in.at[pl.ds(src * 4, 4)]
        to = lax.rem(z + step + 8, 8)
        return copy_to(block, block, b_send.at[k], b_recv.at[src], to * 4 + part, slab)

    block_sends = ((0, 0, 1), (1, 0, -1), (2, -1, 1), (3, 1, -1), (4, -2, 1), (5, 2, -1), (6, -3, 1))

    def wait_block(ahead):
        block_copy(0, ahead, 1).wait_recv()

    def slab_rows(at):
        return x_out.at[:, pl.ds(pl.multiple_of(at * 32, 32), 32)]

    def part_rows(at):
        return x_mid.at[at // 4, :, pl.ds(pl.multiple_of(lax.rem(at, 4) * 8, 8), 8)]

    def y_copy(to):
        return copy_to(slab_rows(to), x_mid.at[slab], y_send.at[to], y_recv.at[slab], dp, to)

    def x_copy(to):
        return copy_to(part_rows(to), x_in.at[dp], x_send.at[to], x_recv.at[dp], to, slab)

    def g_copy(to):
        return copy_to(g_out.at[to], g_in.at[part], g_send.at[to], g_recv.at[part], z * 4 + to, slab)

    own_terms = pltpu.make_async_copy(terms.at[slab], terms_in.at[slab], t_recv.at[slab])
    own_tags = pltpu.make_async_copy(tags, tags_in.at[slab], n_recv.at[slab])
    own_cot = pltpu.make_async_copy(cot.at[part], cot_in.at[dp], c_recv.at[part])
    own_y = pltpu.make_async_copy(slab_rows(slab), x_mid.at[slab], y_recv.at[slab])
    own_x = pltpu.make_async_copy(part_rows(dp), x_in.at[dp], x_recv.at[dp])

    def others(count, me, act):
        def step(i, carry):
            act(lax.rem(me + i, count))
            return carry

        lax.fori_loop(1, count, step, 0)

    barrier = pltpu.get_barrier_semaphore()

    def greet(dp_to, slab_to):
        pl.semaphore_signal(
            barrier, inc=1, device_id=(dp_to, slab_to), device_id_type=pl.DeviceIdType.MESH
        )

    others(8, slab, lambda to: greet(dp, to))
    others(32, dp, lambda to: greet(to, slab))
    pl.semaphore_wait(barrier, 7 + 31)

    own_terms.start()
    own_tags.start()
    own_cot.start()

    def start_slab(to):
        terms_copy(to).start()
        tags_copy(to).start()

    others(4, part, lambda to: cot_copy(to).start())
    others(8, slab, start_slab)
    own_cot.wait()

    def wait_cot(frm):
        copy_to(cot.at[frm], cot_in.at[z * 4 + frm], c_send.at[frm], c_recv.at[frm], z * 4 + frm, slab).wait_recv()

    others(4, part, wait_cot)

    def pass_block(k):
        if k > 1:
            wait_block(block_sends[k][1])
        block_copy(*block_sends[k]).start()

    pass_block(0)
    pass_block(1)

    own_terms.wait()
    own_tags.wait()

    def wait_slab(frm):
        copy_to(terms.at[frm], terms_in.at[frm], t_send.at[frm], t_recv.at[frm], dp, frm).wait_recv()
        copy_to(tags, tags_in.at[frm], n_send.at[frm], n_recv.at[frm], dp, frm).wait_recv()

    others(8, slab, wait_slab)
    pass_block(2)
    pass_block(3)
    t = jnp.concatenate(
        [jnp.concatenate([terms_in[r, e] for r in range(8)], axis=0) for e in range(8)], axis=1
    )
    tag_sum = tags_in[0]
    for r in range(1, 8):
        tag_sum = tag_sum + tags_in[r]
    row = jnp.broadcast_to(tag_sum[0:1, :], (256, 256))
    x = modes_value(row.T.astype(jnp.int32), row.astype(jnp.int32), t, z_hi[...], z_lo[...], xy[...])
    x = swap_rows_runs(x)
    x_out[0] = x[:, :128]
    x_out[1] = x[:, 128:]

    own_y.start()
    others(8, slab, lambda to: y_copy(to).start())
    pass_block(4)
    pass_block(5)

    def pass_on(frm):
        for a in range(4):
            to = frm * 4 + a

            @pl.when(to == dp)
            def _():
                own_x.start()

            @pl.when(to != dp)
            def _():
                x_copy(to).start()

    own_y.wait()
    pass_on(slab)

    def relay(frm):
        copy_to(slab_rows(0), x_mid.at[frm], y_send.at[frm], y_recv.at[frm], dp, frm).wait_recv()
        pass_on(frm)

    others(8, slab, relay)
    pass_block(6)
    for ahead in (3, 4):
        wait_block(ahead)

    def wait_x(frm):
        copy_to(part_rows(0), x_in.at[frm], x_send.at[frm], x_recv.at[frm], frm, slab).wait_recv()

    own_x.wait()
    others(32, dp, wait_x)

    def channels(to):
        both = x_in[:, to // 2]
        pick[...] = jnp.where(lax.rem(to, 2) == 1, pltpu.roll(both, 4, 1), both)
        for o in range(4):
            low = pl.ds(o * 16, 16)
            high = pl.ds(64 + o * 16, 16)

            def sample(s, acc):
                g_low = cot_in[s, low, :].astype(F32)
                g_high = cot_in[s, high, :].astype(F32)
                new = []
                for q in range(4):
                    xq = pick[s, q : q + 1, :]
                    new.append(acc[2 * q] + xq * g_low)
                    new.append(acc[2 * q + 1] + xq * g_high)
                return tuple(new)

            acc = lax.fori_loop(0, 32, sample, tuple(jnp.zeros((16, 128), F32) for _ in range(8)), unroll=8)
            for i in range(2):
                re_low, re_high, im_low, im_high = acc[4 * i : 4 * i + 4]
                fold[i, low, :] = re_low + im_high
                fold[i, high, :] = re_high - im_low
        for i in range(2):
            g_out[to, i] = fold[i].T.astype(BF16)

    def one(k, carry):
        other = (1 - part // 2) * 2 + k
        here = (part // 2) * 2 + lax.rem(part + k + 1, 2)
        to = jnp.where(k < 2, other, here)
        channels(to)

        @pl.when(k < 3)
        def _():
            g_copy(to).start()

        return carry

    lax.fori_loop(0, 4, one, 0)
    out[0, part] = g_out[part, 0]
    out[1, part] = g_out[part, 1]

    def take(frm):
        copy_to(g_out.at[frm], g_in.at[frm], g_send.at[frm], g_recv.at[frm], z * 4 + frm, slab).wait_recv()
        out[0, frm] = g_in[frm, 0]
        out[1, frm] = g_in[frm, 1]

    others(4, part, take)

    def sent_slab(to):
        terms_copy(to).wait_send()
        tags_copy(to).wait_send()

    others(8, slab, sent_slab)
    others(4, part, lambda to: cot_copy(to).wait_send())
    for k in range(7):
        block_copy(*block_sends[k]).wait_send()

    others(8, slab, lambda to: y_copy(to).wait_send())
    others(32, dp, lambda to: x_copy(to).wait_send())
    others(4, part, lambda to: g_copy(to).wait_send())


def exchange(terms, tags, cot):
    z_hi, z_lo, xy = (jnp.asarray(t) for t in tables())
    vm = pl.BlockSpec(memory_space=pltpu.VMEM)
    dma = pltpu.SemaphoreType.DMA
    return pl.pallas_call(
        exchange_kernel,
        out_shape=jax.ShapeDtypeStruct((2, 4, 128, 128), BF16),
        in_specs=[vm] * 6,
        out_specs=vm,
        scratch_shapes=[
            pltpu.VMEM((8, 8, 32, 128), BF16),
            pltpu.VMEM((8, 8, 256), F32),
            pltpu.VMEM((32, 128, 128), BF16),
            pltpu.VMEM((2, 256, 128), F32),
            pltpu.VMEM((8, 2, 32, 128), F32),
            pltpu.VMEM((32, 2, 8, 128), F32),
            pltpu.VMEM((32, 8, 128), F32),
            pltpu.VMEM((4, 2, 128, 128), BF16),
            pltpu.VMEM((4, 2, 128, 128), BF16),
            pltpu.VMEM((2, 128, 128), F32),
            dma((8,)), dma((8,)), dma((8,)), dma((8,)), dma((4,)), dma((4,)), dma((8,)), dma((8,)),
            dma((8,)), dma((8,)), dma((32,)), dma((32,)), dma((4,)), dma((4,)),
        ],
        compiler_params=pltpu.CompilerParams(
            vmem_limit_bytes=VMEM_BYTES, collective_id=0, has_side_effects=True
        ),
        name="exchange",
    )(terms, tags, cot, z_hi, z_lo, xy)


def per_device(
    point_feats, point_coords, slot_block, slot_cell, slot_count, cotangent,
    offset_map, offset_bias, kernel_mix, lift_weight,
):
    terms, tags, cot = lifted_terms(
        slot_block[0, 0].T, slot_cell[0, 0].T, slot_count[0], offset_map.T,
        point_feats[0], point_coords[0].transpose(1, 0, 2), kernel_mix, offset_map.T, offset_bias[None, :], lift_weight,
        cotangent.reshape(512, 128),
    )
    grad = exchange(terms, tags, cot)
    return grad.astype(F32).reshape(2, 2, 16, 16, 128)


def solution(mesh):
    placed = (
        P("dp", "slab", None, None), P("dp", "slab", None, None), P("dp", "slab", None, None),
        P("dp", "slab", None, None), P("dp", "slab", None), P("dp", "slab", None, None, None),
        P(), P(), P(), P(),
    )
    return jax.shard_map(
        per_device,
        mesh=mesh,
        in_specs=placed,
        out_specs=P("dp", "slab", None, None, None),
        check_vma=False,
    )
```
